32 devices in a mesh: seq: 16 (over z, x, core), pipe: 2 (over y).
Axes of the slice: x: 2, y: 2, z: 4, core: 2. Of those that a mesh axis runs over, the one named last changes fastest.
Arguments:
- queries: bfloat16 [2, 32, 2048, 128], P('pipe', None, 'seq'), may hold values from -160 to 160
- key_states: bfloat16 [2, 4, 2048, 128], P('pipe', None, 'seq'), may hold values from -5 to 5
- value_states: bfloat16 [2, 4, 2048, 128], P('pipe', None, 'seq'), may hold values from -6 to 6
- outputs: bfloat16 [2, 32, 2048, 128], P('pipe', None, 'seq'), may hold values from -6 to 6
- out_grads: bfloat16 [2, 32, 2048, 128], P('pipe', None, 'seq'), may hold values from -6 to 6
- selected: int32 [2, 4, 4, 2], P('pipe'), may hold values from 0 to 2, as said below
Outputs:
- grad_queries: bfloat16 [2, 32, 2048, 128], P('pipe', None, 'seq')
- grad_keys: bfloat16 [2, 4, 2048, 128], P('pipe', None, 'seq')
- grad_values: bfloat16 [2, 4, 2048, 128], P('pipe', None, 'seq')
The draws below stay inside these ranges and needn't reach their ends.
Inputs may be any that keep to these rules, and one draw needn't show every extreme that they name: `selected`: for every block b of 2 or more and every key head the two entries are different blocks below b. For block 1 the entries are 0 and 1, for block 0 both are 0. An entry that is not below its block's index stands for no block.
All inputs are finite; a program needn't handle non-finite values.
Results may differ from the reference program's by a relative error of at most 0.009.
Values may be sent and summed in bfloat16 or wider, within the bound.
No kernel may reach another device: no remote copies, remote signals or barrier semaphores. Data moves between devices by JAX's collectives and lax.ppermute only.
A program may use at most 64 MiB of HBM per device.

```python
import jax
import jax.numpy as jnp
from jax import lax

HQ = 32
KVH = 4
DH = 128
BLK = 512
GROUP = 8
PIECE = 64
SECT = 2
TOKENS = 2048
NBLK = 4


def key_base(key):
    raw = jax.random.normal(jax.random.fold_in(key, 11), (SECT, KVH, TOKENS, DH), jnp.float32)
    return jnp.clip(raw, -5.0, 5.0)


def draw_key_states(key, part):
    base = key_base(key)
    return base.astype(jnp.bfloat16)


def draw_queries(key, part):
    raw = jax.random.normal(jax.random.fold_in(key, 21), (SECT, HQ, TOKENS, DH), jnp.float32)
    base = jnp.clip(raw, -5.0, 5.0)
    return base.astype(jnp.bfloat16)


def draw_selected(key, part):
    shape = (SECT, NBLK, KVH)
    block_ids = jnp.arange(NBLK, dtype=jnp.int32)[None, :, None]
    first_raw = jax.random.randint(jax.random.fold_in(key, 31), shape, 0, 1 << 20)
    second_raw = jax.random.randint(jax.random.fold_in(key, 32), shape, 0, 1 << 20)
    first_pick = first_raw % jnp.maximum(block_ids, 1)
    first_pick = jnp.where(block_ids == NBLK - 1, NBLK - 2, first_pick)
    second = second_raw % jnp.maximum(block_ids - 1, 1)
    second = second + (second >= first_pick).astype(jnp.int32)
    second = jnp.where(block_ids >= 2, second, block_ids)
    return jnp.stack([first_pick, second], axis=-1).astype(jnp.int32)


def shard_levels(key, dims, cuts, low, largest):
    level = 1.0
    for axis_at, parts in cuts:
        steps = jax.random.uniform(jax.random.fold_in(jax.random.fold_in(key, 6), axis_at), (parts,), jnp.float32, low / len(cuts), largest / len(cuts))
        level = level * jnp.repeat(jnp.exp(steps), dims[axis_at] // parts).reshape((-1,) + (1,) * (len(dims) - 1 - axis_at))
    return level


def noise(rng, shape, deviation, most, pieces=(), kind=jnp.bfloat16):
    level = shard_levels(rng, shape, pieces, -0.22, 0.18) if pieces else 1.0
    entries = jax.random.normal(rng, shape, jnp.float32) * deviation * level
    return jnp.minimum(jnp.maximum(entries, -most), most).astype(kind)


def setup_inputs(seed: int = 0) -> dict:
    arg_keys = jax.random.split(jax.random.key(seed), 7)
    queries = draw_queries(jax.random.fold_in(arg_keys[6], 71), 0)
    key_states = draw_key_states(jax.random.fold_in(arg_keys[6], 71), 0)
    value_states = noise(arg_keys[2], (SECT, KVH, TOKENS, DH), 1.0, 6.0, ((0, 2), (2, 16)))
    outputs = noise(arg_keys[3], (SECT, HQ, TOKENS, DH), 1.0, 6.0, ((0, 2), (2, 16)))
    out_grads = noise(arg_keys[4], (SECT, HQ, TOKENS, DH), 1.0, 6.0, ((0, 2), (2, 16)))
    selected = draw_selected(jax.random.fold_in(arg_keys[6], 71), 0)
    return dict(queries=queries, key_states=key_states, value_states=value_states, outputs=outputs, out_grads=out_grads, selected=selected)


NEG_FILL = -1e30


def head_backward(query_head, grad_head, output_head, key_head, value_head, chosen):
    scaling = DH ** -0.5
    block_ids = jnp.arange(NBLK, dtype=jnp.int32)
    raw_delta = jnp.sum(grad_head.astype(jnp.float32) * output_head.astype(jnp.float32), axis=-1)
    deltas = lax.optimization_barrier(raw_delta.astype(jnp.bfloat16)).astype(jnp.float32).reshape(NBLK, BLK)
    picks = jnp.concatenate([chosen.astype(jnp.int32), block_ids[:, None]], axis=1)
    key_blocks = key_head.reshape(NBLK, BLK, DH)[picks].reshape(NBLK, 3 * BLK, DH).astype(jnp.float32)
    value_blocks = value_head.reshape(NBLK, BLK, DH)[picks].reshape(NBLK, 3 * BLK, DH).astype(jnp.float32)
    query_blocks = query_head.reshape(NBLK, BLK, DH).astype(jnp.float32)
    grad_blocks = grad_head.reshape(NBLK, BLK, DH).astype(jnp.float32)
    columns = jnp.arange(3 * BLK)
    row_ids = jnp.arange(BLK)
    usable = chosen < block_ids[:, None]
    picked = usable[:, jnp.minimum(columns // BLK, 1)]
    causal = (columns[None, :] - 2 * BLK) <= row_ids[:, None]
    allowed = jnp.where(columns[None, None, :] < 2 * BLK, picked[:, None, :], causal[None, :, :])
    scores = jnp.einsum("bnd,bld->bnl", query_blocks, key_blocks) * scaling
    scores = jnp.where(allowed, scores, NEG_FILL)
    row_max = jnp.max(scores, axis=-1, keepdims=True)
    weights_raw = jnp.exp(scores - row_max)
    probs = weights_raw / jnp.sum(weights_raw, axis=-1, keepdims=True)
    probs_low = probs.astype(jnp.bfloat16).astype(jnp.float32)
    dprobs = jnp.einsum("bnd,bld->bnl", grad_blocks, value_blocks)
    dscores = (probs * (dprobs - deltas[..., None])).astype(jnp.bfloat16).astype(jnp.float32)
    query_grad = (jnp.einsum("bnl,bld->bnd", dscores, key_blocks) * scaling).astype(jnp.bfloat16).reshape(TOKENS, DH)
    split_scores = dscores.reshape(NBLK, 4, 2, PIECE, 3 * BLK)
    split_probs = probs_low.reshape(NBLK, 4, 2, PIECE, 3 * BLK)
    split_query = query_blocks.reshape(NBLK, 4, 2, PIECE, DH)
    split_grad = grad_blocks.reshape(NBLK, 4, 2, PIECE, DH)
    key_terms = jnp.einsum("bkril,bkrid->rbld", split_scores, split_query) * scaling
    value_terms = jnp.einsum("bkril,bkrid->rbld", split_probs, split_grad)
    empty = jnp.zeros((2, NBLK, BLK, DH), jnp.float32)
    key_part = empty.at[:, picks].add(key_terms.reshape(2, NBLK, 3, BLK, DH)).reshape(2, TOKENS, DH)
    value_part = empty.at[:, picks].add(value_terms.reshape(2, NBLK, 3, BLK, DH)).reshape(2, TOKENS, DH)
    return query_grad, key_part.astype(jnp.bfloat16), value_part.astype(jnp.bfloat16)


def section_backward(items):
    queries, key_states, value_states, outputs, out_grads, selected = items

    def per_head(running, head):
        head_group = head // GROUP
        chosen = jnp.take(selected, head_group, axis=1)
        query_grad, key_part, value_part = head_backward(queries[head], out_grads[head], outputs[head], key_states[head_group], value_states[head_group], chosen)
        key_acc, value_acc = running
        key_acc = key_acc.at[head_group].add(jnp.sum(key_part.astype(jnp.float32), axis=0))
        value_acc = value_acc.at[head_group].add(jnp.sum(value_part.astype(jnp.float32), axis=0))
        return (key_acc, value_acc), query_grad

    zeros_init = jnp.zeros((KVH, TOKENS, DH), jnp.float32)
    finals, query_grads = lax.scan(per_head, (zeros_init, zeros_init), jnp.arange(HQ, dtype=jnp.int32))
    return query_grads, finals[0].astype(jnp.bfloat16), finals[1].astype(jnp.bfloat16)


def shift_back(tensor):
    return jnp.concatenate([tensor[1:], jnp.zeros_like(tensor[:1])], axis=0)


def reference(queries, key_states, value_states, outputs, out_grads, selected):
    results = lax.map(section_backward, (queries, key_states, value_states, outputs, out_grads, selected))
    return shift_back(results[0]), shift_back(results[1]), shift_back(results[2])
```

```python
import functools
import math

import jax
import jax.numpy as jnp
from jax import lax
from jax.experimental import pallas as pl
from jax.experimental.pallas import tpu as pltpu
from jax.sharding import PartitionSpec as P

BLK = 512
TILE_HEADS = 2
FAR = 1e30


def nt(a, b):
    return lax.dot_general(a, b, (((1,), (1,)), ((), ())), preferred_element_type=jnp.float32)


def nn(a, b):
    return lax.dot_general(a, b, (((1,), (0,)), ((), ())), preferred_element_type=jnp.float32)


def tn(a, b):
    return lax.dot_general(a, b, (((0,), (0,)), ((), ())), preferred_element_type=jnp.float32)


def attend_kernel(sizes, meta, *refs):
    members, reach, heads, rows, feature = sizes
    take = list(refs)
    queries, grads, deltas = take[:3]
    packs = take[3 : 2 + members]
    take = take[2 + members :]
    near, far = take[0], take[1 : 1 + reach]
    take = take[1 + reach :]
    query_outs, take = take[:members], take[members:]
    far_outs, take = take[:reach], take[reach:]
    (own_out, query_buf, grad_buf, low_buf, delta_buf, pair_buf, key_acc, value_acc, query_done,
     far_done, own_done, blank, in_sem, pair_sem, out_sem) = take
    mine = meta[0]
    offsets = (meta[1], meta[2])
    height = heads * rows
    lanes = TILE_HEADS * rows
    factor = feature ** (-0.5)
    sharp = factor * math.log2(math.e)

    own_copies = []
    for hop in range(members):
        spot = mine ^ hop
        copy = pltpu.make_async_copy(near.at[:, hop], pair_buf.at[2, :, spot], pair_sem.at[2])
        copy.start()
        own_copies.append(copy)
    for slot in range(2):
        for hop in range(reach + 1):
            source = near if hop == 0 else far[hop - 1]

            @pl.when(offsets[slot] == hop)
            def _(source=source, slot=slot):
                pltpu.make_async_copy(source, pair_buf.at[slot], pair_sem.at[slot]).start()

    first = pl.ds(mine * heads, heads)
    piece_copies = []
    for hop in range(members):
        spot = mine ^ hop
        if hop == 0:
            parts = (
                (queries.at[0, first], query_buf.at[spot]),
                (grads.at[0, first], grad_buf.at[spot]),
                (deltas.at[mine], low_buf.at[spot]),
            )
        else:
            pack = packs[hop - 1]
            parts = (
                (pack.at[pl.ds(0, heads)], query_buf.at[spot]),
                (pack.at[pl.ds(heads, heads)], grad_buf.at[spot]),
                (pack.at[2 * heads, pl.ds(0, 16)], low_buf.at[spot]),
            )
        for source, target in parts:
            copy = pltpu.make_async_copy(source, target, in_sem.at[hop])
            copy.start()
            piece_copies.append(copy)
    key_acc[...] = jnp.zeros_like(key_acc)
    value_acc[...] = jnp.zeros_like(value_acc)
    blank[...] = jnp.zeros_like(blank)
    for copy in own_copies:
        copy.wait()
    for slot in range(2):
        pltpu.make_async_copy(near, pair_buf.at[slot], pair_sem.at[slot]).wait()
    for copy in piece_copies:
        copy.wait()
    delta_buf[...] = low_buf[...].astype(jnp.float32)

    biases = [jnp.where(offset > 0, 0.0, FAR) for offset in offsets]
    key_ids = lax.broadcasted_iota(jnp.int32, (rows, lanes), 0)
    row_ids = lax.broadcasted_iota(jnp.int32, (rows, lanes), 1) % rows
    causal = key_ids <= row_ids

    for spot in range(members):
        visible = (spot + 1) * rows

        def tile(step, carry, spot=spot, visible=visible):
            here = pl.ds(step * TILE_HEADS, TILE_HEADS)
            query = query_buf[spot, here].reshape(lanes, feature)
            grad = grad_buf[spot, here].reshape(lanes, feature)
            delta = jnp.concatenate(
                [
                    delta_buf[spot, pl.ds(step * TILE_HEADS + i, 1), :]
                    for i in range(TILE_HEADS)
                ],
                axis=1,
            )
            spans = [(0, BLK), (1, BLK), (2, visible)]

            def fetch(part, slot, length):
                return pair_buf[slot, part].reshape(members * rows, feature)[:length]

            scores = [nt(fetch(0, slot, length), query) for slot, length in spans]
            edge = jnp.where(causal, scores[2][visible - rows :], -FAR)
            scores[2] = (
                edge
                if spot == 0
                else jnp.concatenate([scores[2][: visible - rows], edge], axis=0)
            )
            tops = [jnp.max(score, axis=0, keepdims=True) for score in scores]
            top = jnp.maximum(jnp.maximum(tops[0] - biases[0], tops[1] - biases[1]), tops[2])
            shifts = [top + biases[0], top + biases[1], top]
            raws = [jnp.exp2((score - shift) * sharp) for score, shift in zip(scores, shifts)]
            total = sum(jnp.sum(raw, axis=0, keepdims=True) for raw in raws)
            inverse = 1.0 / total
            query_sum = jnp.zeros((lanes, feature), jnp.float32)
            for (slot, length), raw in zip(spans, raws):
                dprobs = nt(fetch(1, slot, length), grad)
                probs = raw * inverse
                dscores = (probs * (dprobs - delta)).astype(jnp.bfloat16)
                base = slot * BLK
                value_acc[base : base + length] += nn(probs.astype(jnp.bfloat16), grad)
                key_acc[base : base + length] += nn(dscores, query)
                query_sum += tn(dscores, fetch(0, slot, length))
            query_done[spot, here] = (
                (query_sum * factor).astype(jnp.bfloat16).reshape(TILE_HEADS, rows, feature)
            )
            return carry

        lax.fori_loop(0, heads // TILE_HEADS, tile, 0)

    shape = (members, rows, feature)
    for slot in range(2):
        span = slice(slot * BLK, (slot + 1) * BLK)
        far_done[slot, 0] = (key_acc[span] * factor).astype(jnp.bfloat16).reshape(shape)
        far_done[slot, 1] = value_acc[span].astype(jnp.bfloat16).reshape(shape)
    own_done[0] = (key_acc[2 * BLK :] * factor).reshape(shape)
    own_done[1] = value_acc[2 * BLK :].reshape(shape)

    final = []
    for hop in range(1, reach + 1):
        target = far_outs[hop - 1]
        for slot in range(2):

            @pl.when(offsets[slot] == hop)
            def _(target=target, slot=slot):
                pltpu.make_async_copy(far_done.at[slot], target, out_sem.at[hop]).start()

        @pl.when((offsets[0] != hop) & (offsets[1] != hop))
        def _(target=target):
            pltpu.make_async_copy(blank, target, out_sem.at[hop]).start()

        final.append(pltpu.make_async_copy(blank, target, out_sem.at[hop]))
    for hop in range(members):
        spot = mine ^ hop
        for source, target in (
            (own_done.at[:, spot], own_out.at[:, hop]),
            (query_done.at[spot], query_outs[hop]),
        ):
            copy = pltpu.make_async_copy(source, target, out_sem.at[0])
            copy.start()
            final.append(copy)
    for copy in final:
        copy.wait()


def attend(meta, queries, grads, deltas, packs, near, far, sizes):
    members, reach, heads, rows, feature = sizes
    low, wide = jnp.bfloat16, jnp.float32
    pair = (2, members, rows, feature)
    anywhere = pl.BlockSpec(memory_space=pl.ANY)
    outs = (
        [jax.ShapeDtypeStruct((heads, rows, feature), low)] * members
        + [jax.ShapeDtypeStruct(pair, low)] * reach
        + [jax.ShapeDtypeStruct(pair, wide)]
    )
    results = pl.pallas_call(
        functools.partial(attend_kernel, sizes),
        out_shape=outs,
        in_specs=[pl.BlockSpec(memory_space=pltpu.SMEM)]
        + [anywhere] * (3 + len(packs) + 1 + reach),
        out_specs=[anywhere] * len(outs),
        scratch_shapes=[
            pltpu.VMEM((members, heads, rows, feature), low),
            pltpu.VMEM((members, heads, rows, feature), low),
            pltpu.VMEM((members, 16, rows), low),
            pltpu.VMEM((members, 16, rows), wide),
            pltpu.VMEM((3,) + pair, low),
            pltpu.VMEM((3 * BLK, feature), wide),
            pltpu.VMEM((3 * BLK, feature), wide),
            pltpu.VMEM((members, heads, rows, feature), low),
            pltpu.VMEM((2,) + pair, low),
            pltpu.VMEM(pair, wide),
            pltpu.VMEM(pair, low),
            pltpu.SemaphoreType.DMA((members,)),
            pltpu.SemaphoreType.DMA((3,)),
            pltpu.SemaphoreType.DMA((reach + 1,)),
        ],
        compiler_params=pltpu.CompilerParams(vmem_limit_bytes=48 * 1024 * 1024),
    )(meta, queries, grads, deltas, *packs, near, *far)
    return (
        results[:members],
        results[members : members + reach],
        results[members + reach],
    )


def settle_kernel(members, heads, meta, *refs):
    query_parts, pair_parts = refs[:members], refs[members : 2 * members]
    query_out, key_out, value_out, sem = refs[2 * members :]
    mine = meta[0]
    copies = []
    for hop in range(members):
        owner = mine ^ hop
        for source, target in (
            (query_parts[hop], query_out.at[0, pl.ds(owner * heads, heads)]),
            (pair_parts[hop].at[0], key_out.at[0, owner]),
            (pair_parts[hop].at[1], value_out.at[0, owner]),
        ):
            copy = pltpu.make_async_copy(source, target, sem)
            copy.start()
            copies.append(copy)
    for copy in copies:
        copy.wait()


def settle(meta, query_parts, pair_parts, shapes):
    members = len(query_parts)
    heads = query_parts[0].shape[0]
    anywhere = pl.BlockSpec(memory_space=pl.ANY)
    return pl.pallas_call(
        functools.partial(settle_kernel, members, heads),
        out_shape=[jax.ShapeDtypeStruct(shape, jnp.bfloat16) for shape in shapes],
        in_specs=[pl.BlockSpec(memory_space=pltpu.SMEM)] + [anywhere] * (2 * members),
        out_specs=[anywhere] * 3,
        scratch_shapes=[pltpu.SemaphoreType.DMA],
    )(meta, *query_parts, *pair_parts)


def on_device(queries, key_states, value_states, outputs, out_grads, selected):
    devices = lax.axis_size("seq")
    sections = lax.axis_size("pipe")
    head_count, rows, feature = queries.shape[1:]
    key_heads = key_states.shape[1]
    members = BLK // rows
    heads = head_count // key_heads
    reach = devices // members - 1
    assert members == key_heads and members & (members - 1) == 0 and heads <= 16
    rank = lax.axis_index("seq")
    mine = rank % members
    block = rank // members

    def around(tensor, hop):
        return lax.ppermute(tensor, "seq", [(i, i ^ hop) for i in range(devices)])

    def along(tensor, hop):
        step = members * hop
        route = [(i, i + step) for i in range(devices) if 0 <= i + step < devices]
        return lax.ppermute(tensor, "seq", route)

    def previous(tensor, hop):
        route = [
            (i * sections + s, (i ^ hop) * sections + s - 1)
            for i in range(devices)
            for s in range(1, sections)
        ]
        return lax.ppermute(tensor, ("seq", "pipe"), route)

    chosen = lax.dynamic_slice(selected, (0, block, mine, 0), (1, 1, 1, 2)).reshape(2)
    usable = chosen < block
    offsets = jnp.where(usable, block - chosen, 0)
    meta = jnp.concatenate([mine[None], offsets]).astype(jnp.int32)

    pairs = jnp.stack([key_states[0], value_states[0]], axis=0)

    def pair_of(hop):
        return lax.dynamic_index_in_dim(pairs, mine ^ hop, axis=1, keepdims=False)

    pieces = [pair_of(0)] + [around(pair_of(hop), hop) for hop in range(1, members)]
    near = jnp.stack(pieces, axis=1)
    far = [along(near, hop) for hop in range(1, reach + 1)]

    deltas = jnp.sum(
        out_grads[0].astype(jnp.float32) * outputs[0].astype(jnp.float32), axis=-1
    ).astype(jnp.bfloat16)
    deltas = deltas.reshape(key_heads, heads, rows)
    deltas = jnp.pad(deltas, ((0, 0), (0, 16 - heads), (0, 0)))

    packs = []
    for hop in range(1, members):
        other = mine ^ hop
        query_part = lax.dynamic_slice_in_dim(queries[0], other * heads, heads, 0)
        grad_part = lax.dynamic_slice_in_dim(out_grads[0], other * heads, heads, 0)
        delta_part = lax.dynamic_index_in_dim(deltas, other, axis=0, keepdims=True)
        delta_part = jnp.pad(delta_part, ((0, 0), (0, rows - 16), (0, 0)))
        packs.append(around(jnp.concatenate([query_part, grad_part, delta_part], axis=0), hop))

    sizes = (members, reach, heads, rows, feature)
    query_parts, far_parts, own_part = attend(
        meta, queries, out_grads, deltas, packs, near, far, sizes
    )
    query_back = [previous(part, hop) for hop, part in enumerate(query_parts)]
    summed = own_part
    for hop in range(1, reach + 1):
        summed = summed + along(far_parts[hop - 1], -hop).astype(jnp.float32)
    summed = summed.astype(jnp.bfloat16)
    pair_back = [previous(summed[:, hop], hop) for hop in range(members)]
    shapes = (queries.shape, key_states.shape, value_states.shape)
    return tuple(settle(meta, query_back, pair_back, shapes))


def solution(mesh):
    return jax.shard_map(
        on_device,
        mesh=mesh,
        in_specs=(
            P("pipe", None, "seq", None),
            P("pipe", None, "seq", None),
            P("pipe", None, "seq", None),
            P("pipe", None, "seq", None),
            P("pipe", None, "seq", None),
            P("pipe", None, None, None),
        ),
        out_specs=(
            P("pipe", None, "seq", None),
            P("pipe", None, "seq", None),
            P("pipe", None, "seq", None),
        ),
        check_vma=False,
    )
```

```python
import functools
import math

import jax
import jax.numpy as jnp
from jax import lax
from jax.experimental import pallas as pl
from jax.experimental.pallas import tpu as pltpu
from jax.sharding import PartitionSpec as P

BLK = 512
TILE_HEADS = 2
FAR = 1e30


def nt(a, b):
    return lax.dot_general(a, b, (((1,), (1,)), ((), ())), preferred_element_type=jnp.float32)


def nn(a, b):
    return lax.dot_general(a, b, (((1,), (0,)), ((), ())), preferred_element_type=jnp.float32)


def tn(a, b):
    return lax.dot_general(a, b, (((0,), (0,)), ((), ())), preferred_element_type=jnp.float32)


def attend_kernel(sizes, meta, *refs):
    members, reach, heads, rows, feature = sizes
    take = list(refs)
    queries, grads, deltas = take[:3]
    packs = take[3 : 2 + members]
    take = take[2 + members :]
    near, far = take[0], take[1 : 1 + reach]
    take = take[1 + reach :]
    query_outs, take = take[:members], take[members:]
    far_outs, take = take[:reach], take[reach:]
    (own_out, query_buf, grad_buf, low_buf, delta_buf, pair_buf, key_acc, value_acc, query_done,
     far_done, own_done, blank, in_sem, pair_sem, out_sem) = take
    mine = meta[0]
    offsets = (meta[1], meta[2])
    height = heads * rows
    lanes = TILE_HEADS * rows
    factor = feature ** (-0.5)
    sharp = factor * math.log2(math.e)

    own_copies = []
    for hop in range(members):
        spot = mine ^ hop
        copy = pltpu.make_async_copy(near.at[:, hop], pair_buf.at[2, :, spot], pair_sem.at[2])
        copy.start()
        own_copies.append(copy)
    for slot in range(2):
        for hop in range(reach + 1):
            source = near if hop == 0 else far[hop - 1]

            @pl.when(offsets[slot] == hop)
            def _(source=source, slot=slot):
                pltpu.make_async_copy(source, pair_buf.at[slot], pair_sem.at[slot]).start()

    first = pl.ds(mine * heads, heads)
    piece_copies = []
    for hop in range(members):
        spot = mine ^ hop
        if hop == 0:
            parts = (
                (queries.at[0, first], query_buf.at[spot]),
                (grads.at[0, first], grad_buf.at[spot]),
                (deltas.at[mine], low_buf.at[spot]),
            )
        else:
            pack = packs[hop - 1]
            parts = (
                (pack.at[pl.ds(0, heads)], query_buf.at[spot]),
                (pack.at[pl.ds(heads, heads)], grad_buf.at[spot]),
                (pack.at[2 * heads, pl.ds(0, 16)], low_buf.at[spot]),
            )
        for source, target in parts:
            copy = pltpu.make_async_copy(source, target, in_sem.at[hop])
            copy.start()
            piece_copies.append(copy)
    key_acc[...] = jnp.zeros_like(key_acc)
    value_acc[...] = jnp.zeros_like(value_acc)
    blank[...] = jnp.zeros_like(blank)
    for copy in own_copies:
        copy.wait()
    for slot in range(2):
        pltpu.make_async_copy(near, pair_buf.at[slot], pair_sem.at[slot]).wait()
    for copy in piece_copies:
        copy.wait()
    delta_buf[...] = low_buf[...].astype(jnp.float32)

    biases = [jnp.where(offset > 0, 0.0, FAR) for offset in offsets]
    key_ids = lax.broadcasted_iota(jnp.int32, (rows, lanes), 0)
    row_ids = lax.broadcasted_iota(jnp.int32, (rows, lanes), 1) % rows
    causal = key_ids <= row_ids

    for spot in range(members):
        visible = (spot + 1) * rows

        def tile(step, carry, spot=spot, visible=visible):
            here = pl.ds(step * TILE_HEADS, TILE_HEADS)
            query = query_buf[spot, here].reshape(lanes, feature)
            grad = grad_buf[spot, here].reshape(lanes, feature)
            delta = jnp.concatenate(
                [
                    delta_buf[spot, pl.ds(step * TILE_HEADS + i, 1), :]
                    for i in range(TILE_HEADS)
                ],
                axis=1,
            )
            spans = [(0, BLK), (1, BLK), (2, visible)]

            def fetch(part, slot, length):
                return pair_buf[slot, part].reshape(members * rows, feature)[:length]

            scores = [nt(fetch(0, slot, length), query) for slot, length in spans]
            edge = jnp.where(causal, scores[2][visible - rows :], -FAR)
            scores[2] = (
                edge
                if spot == 0
                else jnp.concatenate([scores[2][: visible - rows], edge], axis=0)
            )
            tops = [jnp.max(score, axis=0, keepdims=True) for score in scores]
            top = jnp.maximum(jnp.maximum(tops[0] - biases[0], tops[1] - biases[1]), tops[2])
            shifts = [top + biases[0], top + biases[1], top]
            raws = [jnp.exp2((score - shift) * sharp) for score, shift in zip(scores, shifts)]
            total = sum(jnp.sum(raw, axis=0, keepdims=True) for raw in raws)
            inverse = 1.0 / total
            query_sum = jnp.zeros((lanes, feature), jnp.float32)
            for (slot, length), raw in zip(spans, raws):
                dprobs = nt(fetch(1, slot, length), grad)
                probs = raw * inverse
                dscores = (probs * (dprobs - delta)).astype(jnp.bfloat16)
                base = slot * BLK
                value_acc[base : base + length] += nn(probs.astype(jnp.bfloat16), grad)
                key_acc[base : base + length] += nn(dscores, query)
                query_sum += tn(dscores, fetch(0, slot, length))
            query_done[spot, here] = (
                (query_sum * factor).astype(jnp.bfloat16).reshape(TILE_HEADS, rows, feature)
            )
            return carry

        lax.fori_loop(0, heads // TILE_HEADS, tile, 0)

    shape = (members, rows, feature)
    for slot in range(2):
        span = slice(slot * BLK, (slot + 1) * BLK)
        far_done[slot, 0] = (key_acc[span] * factor).astype(jnp.bfloat16).reshape(shape)
        far_done[slot, 1] = value_acc[span].astype(jnp.bfloat16).reshape(shape)
    own_done[0] = (key_acc[2 * BLK :] * factor).reshape(shape)
    own_done[1] = value_acc[2 * BLK :].reshape(shape)

    final = []
    for hop in range(1, reach + 1):
        target = far_outs[hop - 1]
        for slot in range(2):

            @pl.when(offsets[slot] == hop)
            def _(target=target, slot=slot):
                pltpu.make_async_copy(far_done.at[slot], target, out_sem.at[hop]).start()

        @pl.when((offsets[0] != hop) & (offsets[1] != hop))
        def _(target=target):
            pltpu.make_async_copy(blank, target, out_sem.at[hop]).start()

        final.append(pltpu.make_async_copy(blank, target, out_sem.at[hop]))
    for hop in range(members):
        spot = mine ^ hop
        for source, target in (
            (own_done.at[:, spot], own_out.at[:, hop]),
            (query_done.at[spot], query_outs[hop]),
        ):
            copy = pltpu.make_async_copy(source, target, out_sem.at[0])
            copy.start()
            final.append(copy)
    for copy in final:
        copy.wait()


def attend(meta, queries, grads, deltas, packs, near, far, sizes):
    members, reach, heads, rows, feature = sizes
    low, wide = jnp.bfloat16, jnp.float32
    pair = (2, members, rows, feature)
    anywhere = pl.BlockSpec(memory_space=pl.ANY)
    outs = (
        [jax.ShapeDtypeStruct((heads, rows, feature), low)] * members
        + [jax.ShapeDtypeStruct(pair, low)] * reach
        + [jax.ShapeDtypeStruct(pair, wide)]
    )
    results = pl.pallas_call(
        functools.partial(attend_kernel, sizes),
        out_shape=outs,
        in_specs=[pl.BlockSpec(memory_space=pltpu.SMEM)]
        + [anywhere] * (3 + len(packs) + 1 + reach),
        out_specs=[anywhere] * len(outs),
        scratch_shapes=[
            pltpu.VMEM((members, heads, rows, feature), low),
            pltpu.VMEM((members, heads, rows, feature), low),
            pltpu.VMEM((members, 16, rows), low),
            pltpu.VMEM((members, 16, rows), wide),
            pltpu.VMEM((3,) + pair, low),
            pltpu.VMEM((3 * BLK, feature), wide),
            pltpu.VMEM((3 * BLK, feature), wide),
            pltpu.VMEM((members, heads, rows, feature), low),
            pltpu.VMEM((2,) + pair, low),
            pltpu.VMEM(pair, wide),
            pltpu.VMEM(pair, low),
            pltpu.SemaphoreType.DMA((members,)),
            pltpu.SemaphoreType.DMA((3,)),
            pltpu.SemaphoreType.DMA((reach + 1,)),
        ],
        compiler_params=pltpu.CompilerParams(vmem_limit_bytes=48 * 1024 * 1024),
    )(meta, queries, grads, deltas, *packs, near, *far)
    return (
        results[:members],
        results[members : members + reach],
        results[members + reach],
    )


def settle_kernel(members, heads, meta, *refs):
    query_parts, pair_parts = refs[:members], refs[members : 2 * members]
    query_out, key_out, value_out, sem = refs[2 * members :]
    mine = meta[0]
    copies = []
    for hop in range(members):
        owner = mine ^ hop
        for source, target in (
            (query_parts[hop], query_out.at[0, pl.ds(owner * heads, heads)]),
            (pair_parts[hop].at[0], key_out.at[0, owner]),
            (pair_parts[hop].at[1], value_out.at[0, owner]),
        ):
            copy = pltpu.make_async_copy(source, target, sem)
            copy.start()
            copies.append(copy)
    for copy in copies:
        copy.wait()


def settle(meta, query_parts, pair_parts, shapes):
    members = len(query_parts)
    heads = query_parts[0].shape[0]
    anywhere = pl.BlockSpec(memory_space=pl.ANY)
    return pl.pallas_call(
        functools.partial(settle_kernel, members, heads),
        out_shape=[jax.ShapeDtypeStruct(shape, jnp.bfloat16) for shape in shapes],
        in_specs=[pl.BlockSpec(memory_space=pltpu.SMEM)]
        + [pl.BlockSpec(memory_space=pltpu.VMEM)] * (2 * members),
        out_specs=[anywhere] * 3,
        scratch_shapes=[pltpu.SemaphoreType.DMA],
    )(meta, *query_parts, *pair_parts)


def on_device(queries, key_states, value_states, outputs, out_grads, selected):
    devices = lax.axis_size("seq")
    sections = lax.axis_size("pipe")
    head_count, rows, feature = queries.shape[1:]
    key_heads = key_states.shape[1]
    members = BLK // rows
    heads = head_count // key_heads
    reach = devices // members - 1
    assert members == key_heads and members & (members - 1) == 0 and heads <= 16
    rank = lax.axis_index("seq")
    mine = rank % members
    block = rank // members

    def around(tensor, hop):
        return lax.ppermute(tensor, "seq", [(i, i ^ hop) for i in range(devices)])

    def along(tensor, hop):
        step = members * hop
        route = [(i, i + step) for i in range(devices) if 0 <= i + step < devices]
        return lax.ppermute(tensor, "seq", route)

    def previous(tensor, hop):
        route = [
            (i * sections + s, (i ^ hop) * sections + s - 1)
            for i in range(devices)
            for s in range(1, sections)
        ]
        return lax.ppermute(tensor, ("seq", "pipe"), route)

    chosen = lax.dynamic_slice(selected, (0, block, mine, 0), (1, 1, 1, 2)).reshape(2)
    usable = chosen < block
    offsets = jnp.where(usable, block - chosen, 0)
    meta = jnp.concatenate([mine[None], offsets]).astype(jnp.int32)

    pairs = jnp.stack([key_states[0], value_states[0]], axis=0)

    def pair_of(hop):
        return lax.dynamic_index_in_dim(pairs, mine ^ hop, axis=1, keepdims=False)

    pieces = [pair_of(0)] + [around(pair_of(hop), hop) for hop in range(1, members)]
    near = jnp.stack(pieces, axis=1)
    far = [along(near, hop) for hop in range(1, reach + 1)]

    deltas = jnp.sum(
        out_grads[0].astype(jnp.float32) * outputs[0].astype(jnp.float32), axis=-1
    ).astype(jnp.bfloat16)
    deltas = deltas.reshape(key_heads, heads, rows)
    deltas = jnp.pad(deltas, ((0, 0), (0, 16 - heads), (0, 0)))

    packs = []
    for hop in range(1, members):
        other = mine ^ hop
        query_part = lax.dynamic_slice_in_dim(queries[0], other * heads, heads, 0)
        grad_part = lax.dynamic_slice_in_dim(out_grads[0], other * heads, heads, 0)
        delta_part = lax.dynamic_index_in_dim(deltas, other, axis=0, keepdims=True)
        delta_part = jnp.pad(delta_part, ((0, 0), (0, rows - 16), (0, 0)))
        packs.append(around(jnp.concatenate([query_part, grad_part, delta_part], axis=0), hop))

    sizes = (members, reach, heads, rows, feature)
    query_parts, far_parts, own_part = attend(
        meta, queries, out_grads, deltas, packs, near, far, sizes
    )
    query_back = [previous(part, hop) for hop, part in enumerate(query_parts)]
    summed = own_part
    for hop in range(1, reach + 1):
        summed = summed + along(far_parts[hop - 1], -hop).astype(jnp.float32)
    summed = summed.astype(jnp.bfloat16)
    pair_back = [previous(summed[:, hop], hop) for hop in range(members)]
    shapes = (queries.shape, key_states.shape, value_states.shape)
    return tuple(settle(meta, query_back, pair_back, shapes))


def solution(mesh):
    return jax.shard_map(
        on_device,
        mesh=mesh,
        in_specs=(
            P("pipe", None, "seq", None),
            P("pipe", None, "seq", None),
            P("pipe", None, "seq", None),
            P("pipe", None, "seq", None),
            P("pipe", None, "seq", None),
            P("pipe", None, None, None),
        ),
        out_specs=(
            P("pipe", None, "seq", None),
            P("pipe", None, "seq", None),
            P("pipe", None, "seq", None),
        ),
        check_vma=False,
    )
```

```python
import functools
import math

import jax
import jax.numpy as jnp
from jax import lax
from jax.experimental import pallas as pl
from jax.experimental.pallas import tpu as pltpu
from jax.sharding import PartitionSpec as P

BLK = 512
TILE_HEADS = 2
FAR = 1e30


def nt(a, b):
    return lax.dot_general(a, b, (((1,), (1,)), ((), ())), preferred_element_type=jnp.float32)


def nn(a, b):
    return lax.dot_general(a, b, (((1,), (0,)), ((), ())), preferred_element_type=jnp.float32)


def tn(a, b):
    return lax.dot_general(a, b, (((0,), (0,)), ((), ())), preferred_element_type=jnp.float32)


def attend_kernel(sizes, meta, queries, grads, deltas, pack, pairs, twins, *refs):
    heads, rows, feature = sizes
    (query_outs, pair_keep, pair_give, query_buf, grad_buf, low_buf, delta_buf, pair_buf,
     key_acc, value_acc, query_done, keep_done, give_done, in_sem, out_sem) = (refs[:2],) + refs[2:]
    side, core, head = meta[0], meta[1], meta[2]
    offsets = (meta[3], meta[4])
    lanes = TILE_HEADS * rows
    factor = feature ** (-0.5)
    sharp = factor * math.log2(math.e)

    loads = []
    for hop in range(2):
        spot = 2 * (side ^ hop)
        loads.append((pairs.at[0, :, hop], pair_buf.at[2, :, spot + core]))
        loads.append((twins.at[0, :, hop], pair_buf.at[2, :, spot + 1 - core]))
    for slot in range(2):
        loads.append((pairs.at[offsets[slot]], pair_buf.at[slot, :, pl.ds(0, 2)]))
        loads.append((twins.at[offsets[slot]], pair_buf.at[slot, :, pl.ds(2, 2)]))
    first = pl.ds(head * heads, heads)
    loads.append((queries.at[0, first], query_buf.at[side]))
    loads.append((grads.at[0, first], grad_buf.at[side]))
    loads.append((deltas.at[head], low_buf.at[side]))
    loads.append((pack.at[pl.ds(0, heads)], query_buf.at[1 - side]))
    loads.append((pack.at[pl.ds(heads, heads)], grad_buf.at[1 - side]))
    loads.append((pack.at[2 * heads, pl.ds(0, 16)], low_buf.at[1 - side]))
    copies = [
        pltpu.make_async_copy(source, target, in_sem.at[i])
        for i, (source, target) in enumerate(loads)
    ]
    for copy in copies:
        copy.start()
    key_acc[...] = jnp.zeros_like(key_acc)
    value_acc[...] = jnp.zeros_like(value_acc)
    for copy in copies:
        copy.wait()
    delta_buf[...] = low_buf[...].astype(jnp.float32)

    biases = [jnp.where(offset > 0, 0.0, FAR) for offset in offsets]
    edge_rows = 2 * rows
    key_ids = lax.broadcasted_iota(jnp.int32, (edge_rows, lanes), 0)
    row_ids = lax.broadcasted_iota(jnp.int32, (edge_rows, lanes), 1) % rows
    causal = key_ids <= row_ids + core * rows

    for half in range(2):
        visible = (half + 1) * edge_rows
        spans = [(0, BLK), (1, BLK), (2, visible)]

        def tile(step, carry, half=half, visible=visible, spans=spans):
            here = pl.ds(step * TILE_HEADS, TILE_HEADS)
            query = query_buf[half, here].reshape(lanes, feature)
            grad = grad_buf[half, here].reshape(lanes, feature)
            delta = jnp.concatenate(
                [
                    delta_buf[half, pl.ds(step * TILE_HEADS + i, 1), :]
                    for i in range(TILE_HEADS)
                ],
                axis=1,
            )

            def fetch(part, slot, length):
                return pair_buf[slot, part].reshape(BLK, feature)[:length]

            scores = [nt(fetch(0, slot, length), query) for slot, length in spans]
            edge = jnp.where(causal, scores[2][visible - edge_rows :], -FAR)
            scores[2] = (
                edge
                if half == 0
                else jnp.concatenate([scores[2][: visible - edge_rows], edge], axis=0)
            )
            tops = [jnp.max(score, axis=0, keepdims=True) for score in scores]
            top = jnp.maximum(jnp.maximum(tops[0] - biases[0], tops[1] - biases[1]), tops[2])
            shifts = [top + biases[0], top + biases[1], top]
            raws = [jnp.exp2((score - shift) * sharp) for score, shift in zip(scores, shifts)]
            total = sum(jnp.sum(raw, axis=0, keepdims=True) for raw in raws)
            inverse = 1.0 / total
            query_sum = jnp.zeros((lanes, feature), jnp.float32)
            for (slot, length), raw in zip(spans, raws):
                dprobs = nt(fetch(1, slot, length), grad)
                probs = raw * inverse
                dscores = (probs * (dprobs - delta)).astype(jnp.bfloat16)
                base = slot * BLK
                value_acc[base : base + length] += nn(probs.astype(jnp.bfloat16), grad)
                key_acc[base : base + length] += nn(dscores, query)
                query_sum += tn(dscores, fetch(0, slot, length))
            query_done[half, here] = (
                (query_sum * factor).astype(jnp.bfloat16).reshape(TILE_HEADS, rows, feature)
            )
            return carry

        lax.fori_loop(0, heads // TILE_HEADS, tile, 0)

    stores = [
        (query_done.at[side], query_outs[0]),
        (query_done.at[1 - side], query_outs[1]),
    ]
    shape = (2, rows, feature)
    for part, acc, scale in ((0, key_acc, factor), (1, value_acc, 1.0)):
        for slot in range(2):
            keep = slice(slot * BLK, slot * BLK + 2 * rows)
            give = slice(slot * BLK + 2 * rows, (slot + 1) * BLK)
            keep_done[slot, part] = (acc[keep] * scale).reshape(shape)
            give_done[slot, part] = (acc[give] * scale).astype(jnp.bfloat16).reshape(shape)
        for hop in range(2):
            spot = 2 * (side ^ hop)
            start = pl.multiple_of(2 * BLK + (spot + core) * rows, rows)
            keep_done[2, part, hop] = acc[pl.ds(start, rows)] * scale
            start = pl.multiple_of(2 * BLK + (spot + 1 - core) * rows, rows)
            give_done[2, part, hop] = (acc[pl.ds(start, rows)] * scale).astype(jnp.bfloat16)
    stores += [(keep_done, pair_keep), (give_done, pair_give)]
    copies = [
        pltpu.make_async_copy(source, target, out_sem.at[i])
        for i, (source, target) in enumerate(stores)
    ]
    for copy in copies:
        copy.start()
    for copy in copies:
        copy.wait()


def attend(meta, queries, grads, deltas, pack, pairs, twins, sizes):
    heads, rows, feature = sizes
    low, wide = jnp.bfloat16, jnp.float32
    part = (3, 2, 2, rows, feature)
    anywhere = pl.BlockSpec(memory_space=pl.ANY)
    work = 2 * heads * rows * (2 * BLK + 3 * rows) * feature * 10
    results = pl.pallas_call(
        functools.partial(attend_kernel, sizes),
        out_shape=[jax.ShapeDtypeStruct((heads, rows, feature), low)] * 2
        + [jax.ShapeDtypeStruct(part, wide), jax.ShapeDtypeStruct(part, low)],
        in_specs=[pl.BlockSpec(memory_space=pltpu.SMEM)] + [anywhere] * 6,
        out_specs=[anywhere] * 4,
        scratch_shapes=[
            pltpu.VMEM((2, heads, rows, feature), low),
            pltpu.VMEM((2, heads, rows, feature), low),
            pltpu.VMEM((2, 16, rows), low),
            pltpu.VMEM((2, 16, rows), wide),
            pltpu.VMEM((3, 2, 4, rows, feature), low),
            pltpu.VMEM((3 * BLK, feature), wide),
            pltpu.VMEM((3 * BLK, feature), wide),
            pltpu.VMEM((2, heads, rows, feature), low),
            pltpu.VMEM(part, wide),
            pltpu.VMEM(part, low),
            pltpu.SemaphoreType.DMA((14,)),
            pltpu.SemaphoreType.DMA((4,)),
        ],
        cost_estimate=pl.CostEstimate(
            flops=2 * work,
            bytes_accessed=8 * 1024 * 1024,
            transcendentals=work // (10 * feature),
        ),
        compiler_params=pltpu.CompilerParams(vmem_limit_bytes=48 * 1024 * 1024),
    )(meta, queries, grads, deltas, pack, pairs, twins)
    return results[:2], results[2], results[3]


def settle_kernel(heads, meta, *refs):
    query_parts, pair_parts = refs[:4], refs[4:8]
    query_out, key_out, value_out, sems = refs[8:]
    side = meta[0]
    copies = []
    for chunk in range(2):
        for hop in range(2):
            owner = 2 * (side ^ hop) + chunk
            place = 2 * chunk + hop
            for source, target in (
                (query_parts[place], query_out.at[0, pl.ds(owner * heads, heads)]),
                (pair_parts[place].at[0], key_out.at[0, owner]),
                (pair_parts[place].at[1], value_out.at[0, owner]),
            ):
                copy = pltpu.make_async_copy(source, target, sems.at[len(copies)])
                copy.start()
                copies.append(copy)
    for copy in copies:
        copy.wait()


def settle(meta, query_parts, pair_parts, shapes):
    heads = query_parts[0].shape[0]
    anywhere = pl.BlockSpec(memory_space=pl.ANY)
    return pl.pallas_call(
        functools.partial(settle_kernel, heads),
        out_shape=[jax.ShapeDtypeStruct(shape, jnp.bfloat16) for shape in shapes],
        in_specs=[pl.BlockSpec(memory_space=pltpu.SMEM)]
        + [pl.BlockSpec(memory_space=pltpu.VMEM)] * 8,
        out_specs=[anywhere] * 3,
        scratch_shapes=[pltpu.SemaphoreType.DMA((12,))],
    )(meta, *query_parts, *pair_parts)


def on_device(queries, key_states, value_states, outputs, out_grads, selected):
    devices = lax.axis_size("seq")
    sections = lax.axis_size("pipe")
    head_count, rows, feature = queries.shape[1:]
    key_heads = key_states.shape[1]
    members = BLK // rows
    heads = head_count // key_heads
    reach = devices // members - 1
    assert members == 4 and key_heads == 4 and heads <= 16
    rank = lax.axis_index("seq")
    block = rank // members
    side = rank // 2 % 2
    core = rank % 2

    def around(tensor, hop):
        return lax.ppermute(tensor, "seq", [(i, i ^ hop) for i in range(devices)])

    def along(tensor, hop):
        step = members * hop
        route = [(i, i + step) for i in range(devices) if 0 <= i + step < devices]
        return lax.ppermute(tensor, "seq", route)

    def previous(tensor, hop):
        route = [
            (i * sections + s, (i ^ 2 * hop) * sections + s - 1)
            for i in range(devices)
            for s in range(1, sections)
        ]
        return lax.ppermute(tensor, ("seq", "pipe"), route)

    def offsets_of(head):
        chosen = lax.dynamic_slice(selected, (0, block, head, 0), (1, 1, 1, 2)).reshape(2)
        return jnp.where(chosen < block, block - chosen, 0).astype(jnp.int32)

    offsets = [offsets_of(2 * side + chunk) for chunk in range(2)]

    def pair_of(which):
        return jnp.stack(
            [
                lax.dynamic_slice_in_dim(states[0], 2 * which, 2, 0)
                for states in (key_states, value_states)
            ],
            axis=1,
        )

    mine, other = pair_of(side), around(pair_of(1 - side), 2)
    near = [jnp.stack([mine[chunk], other[chunk]], axis=1) for chunk in range(2)]

    deltas = jnp.sum(
        out_grads[0].astype(jnp.float32) * outputs[0].astype(jnp.float32), axis=-1
    ).astype(jnp.bfloat16)
    deltas = deltas.reshape(key_heads, heads, rows)
    deltas = jnp.pad(deltas, ((0, 0), (0, 16 - heads), (0, 0)))

    def pack_of(head):
        query_part = lax.dynamic_slice_in_dim(queries[0], head * heads, heads, 0)
        grad_part = lax.dynamic_slice_in_dim(out_grads[0], head * heads, heads, 0)
        delta_part = lax.dynamic_index_in_dim(deltas, head, axis=0, keepdims=True)
        delta_part = jnp.pad(delta_part, ((0, 0), (0, rows - 16), (0, 0)))
        return jnp.concatenate([query_part, grad_part, delta_part], axis=0)

    packs = [around(pack_of(2 * (1 - side) + chunk), 2) for chunk in range(2)]
    sizes = (heads, rows, feature)
    query_back, pair_back = [], []
    for chunk in range(2):
        pairs = jnp.stack(
            [near[chunk]] + [along(near[chunk], hop) for hop in range(1, reach + 1)], axis=0
        )
        twins = around(pairs, 1)
        meta = jnp.concatenate([jnp.stack([side, core, 2 * side + chunk]), offsets[chunk]])
        query_parts, keep, give = attend(
            meta, queries, out_grads, deltas, packs[chunk], pairs, twins, sizes
        )
        query_back += [previous(part, hop) for hop, part in enumerate(query_parts)]
        partial = keep + around(give, 1).astype(jnp.float32)
        summed = partial[2]
        for hop in range(1, reach + 1):
            part = jnp.where(
                offsets[chunk][0] == hop,
                partial[0],
                jnp.where(offsets[chunk][1] == hop, partial[1], 0.0),
            )
            summed = summed + along(part.astype(jnp.bfloat16), -hop).astype(jnp.float32)
        summed = summed.astype(jnp.bfloat16)
        pair_back += [previous(summed[:, hop], hop) for hop in range(2)]
    shapes = (queries.shape, key_states.shape, value_states.shape)
    return tuple(settle(jnp.stack([side, core]), query_back, pair_back, shapes))


def solution(mesh):
    return jax.shard_map(
        on_device,
        mesh=mesh,
        in_specs=(
            P("pipe", None, "seq", None),
            P("pipe", None, "seq", None),
            P("pipe", None, "seq", None),
            P("pipe", None, "seq", None),
            P("pipe", None, "seq", None),
            P("pipe", None, None, None),
        ),
        out_specs=(
            P("pipe", None, "seq", None),
            P("pipe", None, "seq", None),
            P("pipe", None, "seq", None),
        ),
        check_vma=False,
    )
```

```python
import functools
import math

import jax
import jax.numpy as jnp
from jax import lax
from jax.experimental import pallas as pl
from jax.experimental.pallas import tpu as pltpu
from jax.sharding import PartitionSpec as P

BLK = 512
TILE_HEADS = 4
FAR = 1e30


def nt(a, b):
    return lax.dot_general(a, b, (((1,), (1,)), ((), ())), preferred_element_type=jnp.float32)


def nn(a, b):
    return lax.dot_general(a, b, (((1,), (0,)), ((), ())), preferred_element_type=jnp.float32)


def tn(a, b):
    return lax.dot_general(a, b, (((0,), (0,)), ((), ())), preferred_element_type=jnp.float32)


def attend_kernel(sizes, first, meta, *refs):
    members, reach, heads, rows, feature = sizes
    take = list(refs)
    if first:
        queries, grads, deltas, pack = take[:4]
        near, far, take = take[4], take[5 : 5 + reach], take[5 + reach :]
        query_outs, acc_outs, take = take[:2], take[2:4], take[4:]
    else:
        packs, acc_ins = take[:2], take[2:4]
        near, far, take = take[4], take[5 : 5 + reach], take[5 + reach :]
        query_outs, take = take[:2], take[2:]
        far_outs, own_out, take = take[:reach], take[reach], take[reach + 1 :]
    query_buf, grad_buf, low_buf, delta_buf, pair_buf, key_acc, value_acc, query_done = take[:8]
    in_sem, pair_sem, out_sem = take[8:11]
    mine = meta[0]
    offsets = (meta[1], meta[2])
    lanes = TILE_HEADS * rows
    factor = feature ** (-0.5)
    sharp = factor * math.log2(math.e)
    group = mine // 2 if first else 1 - mine // 2
    places = [mine % 2, 1 - mine % 2]

    def run(pairs, sems):
        copies = [
            pltpu.make_async_copy(source, target, sems.at[i])
            for i, (source, target) in enumerate(pairs)
        ]
        for copy in copies:
            copy.start()
        return copies

    def of_pack(pack, place):
        return [
            (pack.at[pl.ds(0, heads)], query_buf.at[place]),
            (pack.at[pl.ds(heads, heads)], grad_buf.at[place]),
            (pack.at[2 * heads, pl.ds(0, 16)], low_buf.at[place]),
        ]

    loads = [(near.at[:, hop], pair_buf.at[2, :, mine ^ hop]) for hop in range(members)]
    if first:
        span = pl.ds(mine * heads, heads)
        loads += [
            (queries.at[0, span], query_buf.at[places[0]]),
            (grads.at[0, span], grad_buf.at[places[0]]),
            (deltas.at[mine], low_buf.at[places[0]]),
        ]
        loads += of_pack(pack, places[1])
        key_acc[...] = jnp.zeros_like(key_acc)
        value_acc[...] = jnp.zeros_like(value_acc)
    else:
        loads += of_pack(packs[0], places[0]) + of_pack(packs[1], places[1])
        loads += [(acc_ins[0], key_acc), (acc_ins[1], value_acc)]
    copies = run(loads, in_sem)
    for slot in range(2):
        for hop in range(reach + 1):
            source = near if hop == 0 else far[hop - 1]

            @pl.when(offsets[slot] == hop)
            def _(source=source, slot=slot):
                pltpu.make_async_copy(source, pair_buf.at[slot], pair_sem.at[slot]).start()

    for copy in copies:
        copy.wait()
    for slot in range(2):
        pltpu.make_async_copy(near, pair_buf.at[slot], pair_sem.at[slot]).wait()
    delta_buf[...] = low_buf[...].astype(jnp.float32)

    biases = [jnp.where(offset > 0, 0.0, FAR) for offset in offsets]

    def spans_of(spot):
        return ((0, BLK), (1, BLK), (2, (spot + 1) * rows))

    def fetch(part, slot, length):
        return pair_buf[slot, part].reshape(members * rows, feature)[:length]

    def rows_of(buffer, spot, step):
        span = slice(step * TILE_HEADS, (step + 1) * TILE_HEADS)
        return buffer[spot % 2, span].reshape(lanes, feature)

    def score(spot, step):
        query = rows_of(query_buf, spot, step)
        return [nt(fetch(0, slot, length), query) for slot, length in spans_of(spot)]

    def soften(spot, scores):
        key_ids = lax.broadcasted_iota(jnp.int32, (rows, lanes), 0)
        row_ids = lax.broadcasted_iota(jnp.int32, (rows, lanes), 1) % rows
        fixed = spot * rows
        edge = jnp.where(key_ids <= row_ids, scores[2][fixed:], -FAR)
        scores[2] = jnp.concatenate([scores[2][:fixed], edge], axis=0) if spot else edge
        tops = [jnp.max(part, axis=0, keepdims=True) for part in scores]
        top = jnp.maximum(jnp.maximum(tops[0] - biases[0], tops[1] - biases[1]), tops[2])
        shifts = [top + biases[0], top + biases[1], top]
        raws = [jnp.exp2((part - shift) * sharp) for part, shift in zip(scores, shifts)]
        total = sum(jnp.sum(raw, axis=0, keepdims=True) for raw in raws)
        return raws, 1.0 / total

    def spread(spot, step, raws, inverse):
        query = rows_of(query_buf, spot, step)
        grad = rows_of(grad_buf, spot, step)
        heads_here = range(step * TILE_HEADS, (step + 1) * TILE_HEADS)
        delta = jnp.concatenate([delta_buf[spot % 2, i : i + 1, :] for i in heads_here], axis=1)
        query_sum = jnp.zeros((lanes, feature), jnp.float32)
        for (slot, length), raw in zip(spans_of(spot), raws):
            dprobs = nt(fetch(1, slot, length), grad)
            probs = raw * inverse
            dscores = (probs * (dprobs - delta)).astype(jnp.bfloat16)
            base = slot * BLK
            value_acc[base : base + length] += nn(probs.astype(jnp.bfloat16), grad)
            key_acc[base : base + length] += nn(dscores, query)
            query_sum += tn(dscores, fetch(0, slot, length))
        query_done[spot % 2, step * TILE_HEADS : (step + 1) * TILE_HEADS] = (
            (query_sum * factor).astype(jnp.bfloat16).reshape(TILE_HEADS, rows, feature)
        )

    for half in range(members // 2):

        @pl.when(group == half)
        def _(half=half):
            tiles = [
                (2 * half + spot, step)
                for spot in range(2)
                for step in range(heads // TILE_HEADS)
            ]
            scores = score(*tiles[0])
            for place, tile in enumerate(tiles):
                ahead = score(*tiles[place + 1]) if place + 1 < len(tiles) else None
                raws, inverse = soften(tile[0], scores)
                spread(*tile, raws, inverse)
                scores = ahead

    stores = [(query_done.at[place], out) for place, out in zip(places, query_outs)]
    if first:
        copies = run(stores + [(key_acc, acc_outs[0]), (value_acc, acc_outs[1])], out_sem)
        for copy in copies:
            copy.wait()
        return
    far_done, own_done, blank, far_sem = take[11:]
    copies = run(stores, out_sem)
    blank[...] = jnp.zeros_like(blank)
    shape = (members, rows, feature)
    for slot in range(2):
        span = slice(slot * BLK, (slot + 1) * BLK)
        far_done[slot, 0] = (key_acc[span] * factor).astype(jnp.bfloat16).reshape(shape)
        far_done[slot, 1] = value_acc[span].astype(jnp.bfloat16).reshape(shape)
    for hop in range(1, reach + 1):
        target = far_outs[hop - 1]
        for slot in range(2):

            @pl.when(offsets[slot] == hop)
            def _(target=target, slot=slot, hop=hop):
                pltpu.make_async_copy(far_done.at[slot], target, far_sem.at[hop]).start()

        @pl.when((offsets[0] != hop) & (offsets[1] != hop))
        def _(target=target, hop=hop):
            pltpu.make_async_copy(blank, target, far_sem.at[hop]).start()

    own_done[0] = (key_acc[2 * BLK :] * factor).reshape(shape)
    own_done[1] = value_acc[2 * BLK :].reshape(shape)
    for hop in range(members):
        copy = pltpu.make_async_copy(
            own_done.at[:, mine ^ hop], own_out.at[:, hop], out_sem.at[2 + hop]
        )
        copy.start()
        copies.append(copy)
    for copy in copies:
        copy.wait()
    for hop in range(1, reach + 1):
        pltpu.make_async_copy(blank, far_outs[hop - 1], far_sem.at[hop]).wait()


def attend(meta, inputs, near, far, sizes, first):
    members, reach, heads, rows, feature = sizes
    low, wide = jnp.bfloat16, jnp.float32
    pair = (2, members, rows, feature)
    acc = (3 * BLK, feature)
    anywhere = pl.BlockSpec(memory_space=pl.ANY)
    outs = [jax.ShapeDtypeStruct((heads, rows, feature), low)] * 2
    scratch = [
        pltpu.VMEM((2, heads, rows, feature), low),
        pltpu.VMEM((2, heads, rows, feature), low),
        pltpu.VMEM((2, 16, rows), low),
        pltpu.VMEM((2, 16, rows), wide),
        pltpu.VMEM((3,) + pair, low),
        pltpu.VMEM(acc, wide),
        pltpu.VMEM(acc, wide),
        pltpu.VMEM((2, heads, rows, feature), low),
        pltpu.SemaphoreType.DMA((members + 8,)),
        pltpu.SemaphoreType.DMA((2,)),
        pltpu.SemaphoreType.DMA((members + 2,)),
    ]
    if first:
        outs += [jax.ShapeDtypeStruct(acc, wide)] * 2
    else:
        outs += [jax.ShapeDtypeStruct(pair, low)] * reach + [jax.ShapeDtypeStruct(pair, wide)]
        scratch += [
            pltpu.VMEM((2,) + pair, low),
            pltpu.VMEM(pair, wide),
            pltpu.VMEM(pair, low),
            pltpu.SemaphoreType.DMA((reach + 1,)),
        ]
    work = heads * 2 * rows * (2 * BLK + 3 * rows)
    return pl.pallas_call(
        functools.partial(attend_kernel, sizes, first),
        out_shape=outs,
        in_specs=[pl.BlockSpec(memory_space=pltpu.SMEM)]
        + [anywhere] * (len(inputs) + 1 + reach),
        out_specs=[anywhere] * len(outs),
        scratch_shapes=scratch,
        cost_estimate=pl.CostEstimate(
            flops=10 * work * feature, transcendentals=work, bytes_accessed=6 * 1024 * 1024
        ),
        compiler_params=pltpu.CompilerParams(vmem_limit_bytes=48 * 1024 * 1024),
    )(meta, *inputs, near, *far)


def settle_kernel(members, heads, meta, *refs):
    query_parts, pair_parts = refs[:members], refs[members : 2 * members]
    query_out, key_out, value_out, sem = refs[2 * members :]
    mine = meta[0]
    copies = []
    for hop in range(members):
        owner = mine ^ hop
        for source, target in (
            (query_parts[hop], query_out.at[0, pl.ds(owner * heads, heads)]),
            (pair_parts[hop].at[0], key_out.at[0, owner]),
            (pair_parts[hop].at[1], value_out.at[0, owner]),
        ):
            copy = pltpu.make_async_copy(source, target, sem)
            copy.start()
            copies.append(copy)
    for copy in copies:
        copy.wait()


def settle(meta, query_parts, pair_parts, shapes):
    members = len(query_parts)
    heads = query_parts[0].shape[0]
    anywhere = pl.BlockSpec(memory_space=pl.ANY)
    return pl.pallas_call(
        functools.partial(settle_kernel, members, heads),
        out_shape=[jax.ShapeDtypeStruct(shape, jnp.bfloat16) for shape in shapes],
        in_specs=[pl.BlockSpec(memory_space=pltpu.SMEM)]
        + [pl.BlockSpec(memory_space=pltpu.VMEM)] * (2 * members),
        out_specs=[anywhere] * 3,
        scratch_shapes=[pltpu.SemaphoreType.DMA],
    )(meta, *query_parts, *pair_parts)


def on_device(queries, key_states, value_states, outputs, out_grads, selected):
    devices = lax.axis_size("seq")
    sections = lax.axis_size("pipe")
    head_count, rows, feature = queries.shape[1:]
    key_heads = key_states.shape[1]
    members = BLK // rows
    heads = head_count // key_heads
    reach = devices // members - 1
    assert members == 4 and key_heads == 4 and heads <= 16
    rank = lax.axis_index("seq")
    mine = rank % members
    block = rank // members

    def around(tensor, hop):
        return lax.ppermute(tensor, "seq", [(i, i ^ hop) for i in range(devices)])

    def along(tensor, hop):
        step = members * hop
        route = [(i, i + step) for i in range(devices) if 0 <= i + step < devices]
        return lax.ppermute(tensor, "seq", route)

    def previous(tensor, hop):
        route = [
            (i * sections + s, (i ^ hop) * sections + s - 1)
            for i in range(devices)
            for s in range(1, sections)
        ]
        return lax.ppermute(tensor, ("seq", "pipe"), route)

    chosen = lax.dynamic_slice(selected, (0, block, mine, 0), (1, 1, 1, 2)).reshape(2)
    usable = chosen < block
    offsets = jnp.where(usable, block - chosen, 0)
    meta = jnp.concatenate([mine[None], offsets]).astype(jnp.int32)

    def pair_of(hop):
        return jnp.concatenate(
            [
                lax.dynamic_slice_in_dim(states[0], mine ^ hop, 1, 0)
                for states in (key_states, value_states)
            ],
            axis=0,
        )

    deltas = jnp.sum(
        out_grads[0].astype(jnp.float32) * outputs[0].astype(jnp.float32), axis=-1
    ).astype(jnp.bfloat16)
    deltas = deltas.reshape(key_heads, heads, rows)
    deltas = jnp.pad(deltas, ((0, 0), (0, 16 - heads), (0, 0)))

    def pack_of(hop):
        other = mine ^ hop
        query_part = lax.dynamic_slice_in_dim(queries[0], other * heads, heads, 0)
        grad_part = lax.dynamic_slice_in_dim(out_grads[0], other * heads, heads, 0)
        delta_part = lax.dynamic_index_in_dim(deltas, other, axis=0, keepdims=True)
        delta_part = jnp.pad(delta_part, ((0, 0), (0, rows - 16), (0, 0)))
        extra = [pair_of(hop)] if hop == 1 else []
        return jnp.concatenate([query_part, grad_part, delta_part] + extra, axis=0)

    sides = [around(pair_of(hop), hop) for hop in range(2, members)]
    packs = [around(pack_of(hop), hop) for hop in range(1, members)]
    pieces = [pair_of(0), packs[0][2 * heads + 1 :]] + sides
    near = jnp.stack(pieces, axis=1)
    far = [along(near, hop) for hop in range(1, reach + 1)]

    sizes = (members, reach, heads, rows, feature)
    inputs = [queries, out_grads, deltas, packs[0]]
    *early_parts, key_acc, value_acc = attend(meta, inputs, near, far, sizes, True)
    early = [previous(part, hop) for hop, part in enumerate(early_parts)]
    inputs = [packs[1], packs[2], key_acc, value_acc]
    results = attend(meta, inputs, near, far, sizes, False)
    late_parts, far_parts, own_part = results[:2], results[2:-1], results[-1]
    early, late_parts, far_parts = lax.optimization_barrier((early, late_parts, far_parts))
    far_back = [along(part, -hop - 1) for hop, part in enumerate(far_parts)]
    late = [previous(part, hop + 2) for hop, part in enumerate(late_parts)]
    summed = own_part
    for part in far_back:
        summed = summed + part.astype(jnp.float32)
    summed = summed.astype(jnp.bfloat16)
    pair_back = [previous(summed[:, hop], hop) for hop in range(members)]
    shapes = (queries.shape, key_states.shape, value_states.shape)
    return tuple(settle(meta, early + late, pair_back, shapes))


def solution(mesh):
    return jax.shard_map(
        on_device,
        mesh=mesh,
        in_specs=(
            P("pipe", None, "seq", None),
            P("pipe", None, "seq", None),
            P("pipe", None, "seq", None),
            P("pipe", None, "seq", None),
            P("pipe", None, "seq", None),
            P("pipe", None, None, None),
        ),
        out_specs=(
            P("pipe", None, "seq", None),
            P("pipe", None, "seq", None),
            P("pipe", None, "seq", None),
        ),
        check_vma=False,
    )
```

```python
import functools
import math

import jax
import jax.numpy as jnp
from jax import lax
from jax.experimental import pallas as pl
from jax.experimental.pallas import tpu as pltpu
from jax.sharding import PartitionSpec as P

BLK = 512
TILE_HEADS = 4
FAR = 1e30


def nt(a, b):
    return lax.dot_general(a, b, (((1,), (1,)), ((), ())), preferred_element_type=jnp.float32)


def nn(a, b):
    return lax.dot_general(a, b, (((1,), (0,)), ((), ())), preferred_element_type=jnp.float32)


def tn(a, b):
    return lax.dot_general(a, b, (((0,), (0,)), ((), ())), preferred_element_type=jnp.float32)


def attend_kernel(sizes, first, meta, *refs):
    members, reach, heads, rows, feature = sizes
    take = list(refs)
    if first:
        queries, grads, deltas, pack = take[:4]
        near, far, take = take[4], take[5 : 5 + reach], take[5 + reach :]
        query_outs, acc_outs, take = take[:2], take[2:4], take[4:]
    else:
        packs, acc_ins = take[:2], take[2:4]
        near, far, take = take[4], take[5 : 5 + reach], take[5 + reach :]
        query_outs, take = take[:2], take[2:]
        far_outs, own_out, take = take[:reach], take[reach], take[reach + 1 :]
    query_buf, grad_buf, low_buf, delta_buf, pair_buf, key_acc, value_acc, query_done = take[:8]
    in_sem, pair_sem, out_sem = take[8:11]
    mine = meta[0]
    offsets = (meta[1], meta[2])
    lanes = TILE_HEADS * rows
    factor = feature ** (-0.5)
    sharp = factor * math.log2(math.e)
    group = mine // 2 if first else 1 - mine // 2
    places = [mine % 2, 1 - mine % 2]

    def run(pairs, sems):
        copies = [
            pltpu.make_async_copy(source, target, sems.at[i])
            for i, (source, target) in enumerate(pairs)
        ]
        for copy in copies:
            copy.start()
        return copies

    def of_pack(pack, place):
        return [
            (pack.at[pl.ds(0, heads)], query_buf.at[place]),
            (pack.at[pl.ds(heads, heads)], grad_buf.at[place]),
            (pack.at[2 * heads, pl.ds(0, 16)], low_buf.at[place]),
        ]

    loads = [(near.at[:, hop], pair_buf.at[2, :, mine ^ hop]) for hop in range(members)]
    if first:
        span = pl.ds(mine * heads, heads)
        loads += [
            (queries.at[0, span], query_buf.at[places[0]]),
            (grads.at[0, span], grad_buf.at[places[0]]),
            (deltas.at[mine], low_buf.at[places[0]]),
        ]
        loads += of_pack(pack, places[1])
        key_acc[...] = jnp.zeros_like(key_acc)
        value_acc[...] = jnp.zeros_like(value_acc)
    else:
        loads += of_pack(packs[0], places[0]) + of_pack(packs[1], places[1])
        loads += [(acc_ins[0], key_acc), (acc_ins[1], value_acc)]
    copies = run(loads, in_sem)
    for slot in range(2):
        for hop in range(reach + 1):
            source = near if hop == 0 else far[hop - 1]

            @pl.when(offsets[slot] == hop)
            def _(source=source, slot=slot):
                pltpu.make_async_copy(source, pair_buf.at[slot], pair_sem.at[slot]).start()

    for copy in copies:
        copy.wait()
    for slot in range(2):
        pltpu.make_async_copy(near, pair_buf.at[slot], pair_sem.at[slot]).wait()
    delta_buf[...] = low_buf[...].astype(jnp.float32)

    biases = [jnp.where(offset > 0, 0.0, FAR) for offset in offsets]

    steps = heads // TILE_HEADS
    edge_rows = 2 * rows

    def spans_of(half):
        return ((0, BLK), (1, BLK), (2, (half + 1) * edge_rows))

    def fetch(part, slot, length):
        return pair_buf[slot, part].reshape(members * rows, feature)[:length]

    def rows_of(buffer, place, step):
        return buffer[place, pl.ds(step * TILE_HEADS, TILE_HEADS)].reshape(lanes, feature)

    def score(half, place, step):
        query = rows_of(query_buf, place, step)
        return [nt(fetch(0, slot, length), query) for slot, length in spans_of(half)]

    def soften(half, place, scores):
        key_ids = lax.broadcasted_iota(jnp.int32, (edge_rows, lanes), 0)
        row_ids = lax.broadcasted_iota(jnp.int32, (edge_rows, lanes), 1) % rows
        fixed = half * edge_rows
        edge = jnp.where(key_ids <= row_ids + place * rows, scores[2][fixed:], -FAR)
        scores[2] = jnp.concatenate([scores[2][:fixed], edge], axis=0) if half else edge
        tops = [jnp.max(part, axis=0, keepdims=True) for part in scores]
        top = jnp.maximum(jnp.maximum(tops[0] - biases[0], tops[1] - biases[1]), tops[2])
        shifts = [top + biases[0], top + biases[1], top]
        raws = [jnp.exp2((part - shift) * sharp) for part, shift in zip(scores, shifts)]
        total = sum(jnp.sum(raw, axis=0, keepdims=True) for raw in raws)
        return raws, 1.0 / total

    def spread(half, place, step, raws, inverse):
        query = rows_of(query_buf, place, step)
        grad = rows_of(grad_buf, place, step)
        delta = jnp.concatenate(
            [
                delta_buf[place, pl.ds(step * TILE_HEADS + i, 1), :]
                for i in range(TILE_HEADS)
            ],
            axis=1,
        )
        query_sum = jnp.zeros((lanes, feature), jnp.float32)
        for (slot, length), raw in zip(spans_of(half), raws):
            dprobs = nt(fetch(1, slot, length), grad)
            probs = raw * inverse
            dscores = (probs * (dprobs - delta)).astype(jnp.bfloat16)
            base = slot * BLK
            value_acc[base : base + length] += nn(probs.astype(jnp.bfloat16), grad)
            key_acc[base : base + length] += nn(dscores, query)
            query_sum += tn(dscores, fetch(0, slot, length))
        query_done[place, pl.ds(step * TILE_HEADS, TILE_HEADS)] = (
            (query_sum * factor).astype(jnp.bfloat16).reshape(TILE_HEADS, rows, feature)
        )

    for half in range(members // 2):

        @pl.when(group == half)
        def _(half=half):
            def tile(index, carry, half=half):
                place, step = index // steps, index % steps
                raws, inverse = soften(half, place, score(half, place, step))
                spread(half, place, step, raws, inverse)
                return carry

            lax.fori_loop(0, 2 * steps, tile, 0)

    stores = [(query_done.at[place], out) for place, out in zip(places, query_outs)]
    if first:
        copies = run(stores + [(key_acc, acc_outs[0]), (value_acc, acc_outs[1])], out_sem)
        for copy in copies:
            copy.wait()
        return
    far_done, own_done, blank, far_sem = take[11:]
    copies = run(stores, out_sem)
    blank[...] = jnp.zeros_like(blank)
    shape = (members, rows, feature)
    for slot in range(2):
        span = slice(slot * BLK, (slot + 1) * BLK)
        far_done[slot, 0] = (key_acc[span] * factor).astype(jnp.bfloat16).reshape(shape)
        far_done[slot, 1] = value_acc[span].astype(jnp.bfloat16).reshape(shape)
    for hop in range(1, reach + 1):
        target = far_outs[hop - 1]
        for slot in range(2):

            @pl.when(offsets[slot] == hop)
            def _(target=target, slot=slot, hop=hop):
                pltpu.make_async_copy(far_done.at[slot], target, far_sem.at[hop]).start()

        @pl.when((offsets[0] != hop) & (offsets[1] != hop))
        def _(target=target, hop=hop):
            pltpu.make_async_copy(blank, target, far_sem.at[hop]).start()

    own_done[0] = (key_acc[2 * BLK :] * factor).reshape(shape)
    own_done[1] = value_acc[2 * BLK :].reshape(shape)
    for hop in range(members):
        copy = pltpu.make_async_copy(
            own_done.at[:, mine ^ hop], own_out.at[:, hop], out_sem.at[2 + hop]
        )
        copy.start()
        copies.append(copy)
    for copy in copies:
        copy.wait()
    for hop in range(1, reach + 1):
        pltpu.make_async_copy(blank, far_outs[hop - 1], far_sem.at[hop]).wait()


def attend(meta, inputs, near, far, sizes, first):
    members, reach, heads, rows, feature = sizes
    low, wide = jnp.bfloat16, jnp.float32
    pair = (2, members, rows, feature)
    acc = (3 * BLK, feature)
    anywhere = pl.BlockSpec(memory_space=pl.ANY)
    outs = [jax.ShapeDtypeStruct((heads, rows, feature), low)] * 2
    scratch = [
        pltpu.VMEM((2, heads, rows, feature), low),
        pltpu.VMEM((2, heads, rows, feature), low),
        pltpu.VMEM((2, 16, rows), low),
        pltpu.VMEM((2, 16, rows), wide),
        pltpu.VMEM((3,) + pair, low),
        pltpu.VMEM(acc, wide),
        pltpu.VMEM(acc, wide),
        pltpu.VMEM((2, heads, rows, feature), low),
        pltpu.SemaphoreType.DMA((members + 8,)),
        pltpu.SemaphoreType.DMA((2,)),
        pltpu.SemaphoreType.DMA((members + 2,)),
    ]
    if first:
        outs += [jax.ShapeDtypeStruct(acc, wide)] * 2
    else:
        outs += [jax.ShapeDtypeStruct(pair, low)] * reach + [jax.ShapeDtypeStruct(pair, wide)]
        scratch += [
            pltpu.VMEM((2,) + pair, low),
            pltpu.VMEM(pair, wide),
            pltpu.VMEM(pair, low),
            pltpu.SemaphoreType.DMA((reach + 1,)),
        ]
    work = heads * 2 * rows * (2 * BLK + 3 * rows)
    return pl.pallas_call(
        functools.partial(attend_kernel, sizes, first),
        out_shape=outs,
        in_specs=[pl.BlockSpec(memory_space=pltpu.SMEM)]
        + [anywhere] * (len(inputs) + 1 + reach),
        out_specs=[anywhere] * len(outs),
        scratch_shapes=scratch,
        cost_estimate=pl.CostEstimate(
            flops=10 * work * feature, transcendentals=work, bytes_accessed=6 * 1024 * 1024
        ),
        compiler_params=pltpu.CompilerParams(vmem_limit_bytes=48 * 1024 * 1024),
    )(meta, *inputs, near, *far)


def settle_kernel(members, heads, meta, *refs):
    query_parts, pair_parts = refs[:members], refs[members : 2 * members]
    query_out, key_out, value_out, sem = refs[2 * members :]
    mine = meta[0]
    copies = []
    for hop in range(members):
        owner = mine ^ hop
        for source, target in (
            (query_parts[hop], query_out.at[0, pl.ds(owner * heads, heads)]),
            (pair_parts[hop].at[0], key_out.at[0, owner]),
            (pair_parts[hop].at[1], value_out.at[0, owner]),
        ):
            copy = pltpu.make_async_copy(source, target, sem)
            copy.start()
            copies.append(copy)
    for copy in copies:
        copy.wait()


def settle(meta, query_parts, pair_parts, shapes):
    members = len(query_parts)
    heads = query_parts[0].shape[0]
    anywhere = pl.BlockSpec(memory_space=pl.ANY)
    return pl.pallas_call(
        functools.partial(settle_kernel, members, heads),
        out_shape=[jax.ShapeDtypeStruct(shape, jnp.bfloat16) for shape in shapes],
        in_specs=[pl.BlockSpec(memory_space=pltpu.SMEM)]
        + [pl.BlockSpec(memory_space=pltpu.VMEM)] * (2 * members),
        out_specs=[anywhere] * 3,
        scratch_shapes=[pltpu.SemaphoreType.DMA],
    )(meta, *query_parts, *pair_parts)


def on_device(queries, key_states, value_states, outputs, out_grads, selected):
    devices = lax.axis_size("seq")
    sections = lax.axis_size("pipe")
    head_count, rows, feature = queries.shape[1:]
    key_heads = key_states.shape[1]
    members = BLK // rows
    heads = head_count // key_heads
    reach = devices // members - 1
    assert members == 4 and key_heads == 4 and heads <= 16
    rank = lax.axis_index("seq")
    mine = rank % members
    block = rank // members

    def around(tensor, hop):
        return lax.ppermute(tensor, "seq", [(i, i ^ hop) for i in range(devices)])

    def along(tensor, hop):
        step = members * hop
        route = [(i, i + step) for i in range(devices) if 0 <= i + step < devices]
        return lax.ppermute(tensor, "seq", route)

    def previous(tensor, hop):
        route = [
            (i * sections + s, (i ^ hop) * sections + s - 1)
            for i in range(devices)
            for s in range(1, sections)
        ]
        return lax.ppermute(tensor, ("seq", "pipe"), route)

    chosen = lax.dynamic_slice(selected, (0, block, mine, 0), (1, 1, 1, 2)).reshape(2)
    usable = chosen < block
    offsets = jnp.where(usable, block - chosen, 0)
    meta = jnp.concatenate([mine[None], offsets]).astype(jnp.int32)

    def pair_of(hop):
        return jnp.concatenate(
            [
                lax.dynamic_slice_in_dim(states[0], mine ^ hop, 1, 0)
                for states in (key_states, value_states)
            ],
            axis=0,
        )

    deltas = jnp.sum(
        out_grads[0].astype(jnp.float32) * outputs[0].astype(jnp.float32), axis=-1
    ).astype(jnp.bfloat16)
    deltas = deltas.reshape(key_heads, heads, rows)
    deltas = jnp.pad(deltas, ((0, 0), (0, 16 - heads), (0, 0)))

    def pack_of(hop):
        other = mine ^ hop
        query_part = lax.dynamic_slice_in_dim(queries[0], other * heads, heads, 0)
        grad_part = lax.dynamic_slice_in_dim(out_grads[0], other * heads, heads, 0)
        extra = lax.dynamic_index_in_dim(deltas, other, axis=0, keepdims=True)
        extra = jnp.pad(extra, ((0, 0), (0, rows - 16), (0, 0)))
        if hop == 1:
            extra = lax.optimization_barrier(jnp.concatenate([extra, pair_of(hop)], axis=0))
        return jnp.concatenate([query_part, grad_part, extra], axis=0)

    sides = [around(pair_of(hop), hop) for hop in range(2, members)]
    packs = [around(pack_of(hop), hop) for hop in range(1, members)]
    pieces = [pair_of(0), packs[0][2 * heads + 1 :]] + sides
    near = jnp.stack(pieces, axis=1)
    far = [along(near, hop) for hop in range(1, reach + 1)]

    sizes = (members, reach, heads, rows, feature)
    inputs = [queries, out_grads, deltas, packs[0]]
    *early_parts, key_acc, value_acc = attend(meta, inputs, near, far, sizes, True)
    early = [previous(part, hop) for hop, part in enumerate(early_parts)]
    inputs = [packs[1], packs[2], key_acc, value_acc]
    results = attend(meta, inputs, near, far, sizes, False)
    late_parts, far_parts, own_part = results[:2], results[2:-1], results[-1]
    early, late_parts, far_parts = lax.optimization_barrier((early, late_parts, far_parts))
    far_back = [along(part, -hop - 1) for hop, part in enumerate(far_parts)]
    late = [previous(part, hop + 2) for hop, part in enumerate(late_parts)]
    summed = own_part
    for part in far_back:
        summed = summed + part.astype(jnp.float32)
    summed = summed.astype(jnp.bfloat16)
    pair_back = [previous(summed[:, hop], hop) for hop in range(members)]
    shapes = (queries.shape, key_states.shape, value_states.shape)
    return tuple(settle(meta, early + late, pair_back, shapes))


def solution(mesh):
    return jax.shard_map(
        on_device,
        mesh=mesh,
        in_specs=(
            P("pipe", None, "seq", None),
            P("pipe", None, "seq", None),
            P("pipe", None, "seq", None),
            P("pipe", None, "seq", None),
            P("pipe", None, "seq", None),
            P("pipe", None, None, None),
        ),
        out_specs=(
            P("pipe", None, "seq", None),
            P("pipe", None, "seq", None),
            P("pipe", None, "seq", None),
        ),
        check_vma=False,
    )
```

```python
import functools
import math

import jax
import jax.numpy as jnp
from jax import lax
from jax.experimental import pallas as pl
from jax.experimental.pallas import tpu as pltpu
from jax.sharding import PartitionSpec as P

BLK = 512
TILE_HEADS = 2
CHUNK = 256
FAR = 1e30


def nt(a, b):
    return lax.dot_general(a, b, (((1,), (1,)), ((), ())), preferred_element_type=jnp.float32)


def nn(a, b):
    return lax.dot_general(a, b, (((1,), (0,)), ((), ())), preferred_element_type=jnp.float32)


def tn(a, b):
    return lax.dot_general(a, b, (((0,), (0,)), ((), ())), preferred_element_type=jnp.float32)


def attend_kernel(sizes, first, meta, *refs):
    members, reach, heads, rows, feature = sizes
    take = list(refs)
    if first:
        queries, grads, deltas, pack = take[:4]
        near, far, take = take[4], take[5 : 5 + reach], take[5 + reach :]
        query_outs, acc_outs, take = take[:2], take[2:4], take[4:]
    else:
        packs, acc_ins = take[:2], take[2:4]
        near, far, take = take[4], take[5 : 5 + reach], take[5 + reach :]
        query_outs, take = take[:2], take[2:]
        far_outs, own_out, take = take[:reach], take[reach], take[reach + 1 :]
    query_buf, grad_buf, low_buf, delta_buf, pair_buf, key_acc, value_acc, query_done = take[:8]
    in_sem, pair_sem, out_sem, even, odd, dprobs_buf, turned = take[8:15]
    mine = meta[0]
    offsets = (meta[1], meta[2])
    lanes = TILE_HEADS * rows
    factor = feature ** (-0.5)
    sharp = factor * math.log2(math.e)
    group = mine // 2 if first else 1 - mine // 2
    places = [mine % 2, 1 - mine % 2]

    def run(pairs, sems):
        copies = [
            pltpu.make_async_copy(source, target, sems.at[i])
            for i, (source, target) in enumerate(pairs)
        ]
        for copy in copies:
            copy.start()
        return copies

    def of_pack(pack, place):
        return [
            (pack.at[pl.ds(0, heads)], query_buf.at[place]),
            (pack.at[pl.ds(heads, heads)], grad_buf.at[place]),
            (pack.at[2 * heads, pl.ds(0, heads)], low_buf.at[place]),
        ]

    loads = [(near.at[:, hop], pair_buf.at[2, :, mine ^ hop]) for hop in range(members)]
    if first:
        span = pl.ds(mine * heads, heads)
        loads += [
            (queries.at[0, span], query_buf.at[places[0]]),
            (grads.at[0, span], grad_buf.at[places[0]]),
            (deltas.at[mine], low_buf.at[places[0]]),
        ]
        loads += of_pack(pack, places[1])
        key_acc[...] = jnp.zeros_like(key_acc)
        value_acc[...] = jnp.zeros_like(value_acc)
    else:
        loads += of_pack(packs[0], places[0]) + of_pack(packs[1], places[1])
        loads += [(acc_ins[0], key_acc), (acc_ins[1], value_acc)]
    copies = run(loads, in_sem)
    for slot in range(2):
        for hop in range(reach + 1):
            source = near if hop == 0 else far[hop - 1]

            @pl.when(offsets[slot] == hop)
            def _(source=source, slot=slot):
                pltpu.make_async_copy(source, pair_buf.at[slot], pair_sem.at[slot]).start()

    for copy in copies:
        copy.wait()
    for slot in range(2):
        pltpu.make_async_copy(near, pair_buf.at[slot], pair_sem.at[slot]).wait()
    delta_buf[...] = low_buf[...].astype(jnp.float32)

    biases = [jnp.where(offset > 0, 0.0, FAR) for offset in offsets]

    steps = heads // TILE_HEADS
    edge_rows = 2 * rows
    for slot in range(3):
        turned[slot] = pair_buf[slot, 0].reshape(BLK, feature).T

    def fetch(part, slot, start, size):
        return pair_buf[slot, part].reshape(BLK, feature)[start : start + size]

    def rows_of(buffer, place, step):
        return buffer[place, pl.ds(step * TILE_HEADS, TILE_HEADS)].reshape(lanes, feature)

    def score(half, index, buffer, span, tops):
        slot, start, size = span
        place, step = index // steps, index % steps
        part = nt(fetch(0, slot, start, size), rows_of(query_buf, place, step))
        if slot == 2 and start + size > half * edge_rows:
            key_ids = lax.broadcasted_iota(jnp.int32, (size, lanes), 0) + start
            row_ids = lax.broadcasted_iota(jnp.int32, (size, lanes), 1) % rows
            part = jnp.where(key_ids <= row_ids + (2 * half + place) * rows, part, -FAR)
        base = slot * BLK + start
        buffer[base : base + size] = part
        tops[slot] = jnp.maximum(tops[slot], jnp.max(part, axis=0, keepdims=True))

    def tile(half, index, tops, now, later):
        place, step = index // steps, index % steps
        query = rows_of(query_buf, place, step)
        grad = rows_of(grad_buf, place, step)
        delta = jnp.concatenate(
            [
                delta_buf[place, pl.ds(step * TILE_HEADS + i, 1), :]
                for i in range(TILE_HEADS)
            ],
            axis=1,
        )
        spans = spans_of(half)
        top = jnp.maximum(jnp.maximum(tops[0] - biases[0], tops[1] - biases[1]), tops[2])
        shifts = [top + biases[0], top + biases[1], top]
        total = jnp.zeros((1, lanes), jnp.float32)
        fresh = [jnp.full((1, lanes), -FAR, jnp.float32)] * 3
        for span in spans:
            slot, start, size = span
            base = slot * BLK + start
            score(half, jnp.minimum(index + 1, 2 * steps - 1), later, span, fresh)
            dprobs_buf[base : base + size] = nt(fetch(1, slot, start, size), grad)
            raw = jnp.exp2((now[base : base + size] - shifts[slot]) * sharp)
            now[base : base + size] = raw
            total += jnp.sum(raw, axis=0, keepdims=True)
        inverse = 1.0 / total
        query_sum = jnp.zeros((feature, lanes), jnp.float32)
        held = None
        for span in spans + [None]:
            if span is not None:
                slot, start, size = span
                base = slot * BLK + start
                probs = now[base : base + size] * inverse
                dscores = (probs * (dprobs_buf[base : base + size] - delta)).astype(jnp.bfloat16)
                waiting = (base, size, slot, start, probs.astype(jnp.bfloat16), dscores)
            if held is not None:
                base, size, slot, start, probs_low, dscores = held
                value_acc[base : base + size] += nn(probs_low, grad)
                key_acc[base : base + size] += nn(dscores, query)
                query_sum += nn(turned[slot][:, start : start + size], dscores)
            held = waiting
        query_done[place, pl.ds(step * TILE_HEADS, TILE_HEADS)] = (
            (query_sum.T * factor).astype(jnp.bfloat16).reshape(TILE_HEADS, rows, feature)
        )
        return fresh

    def spans_of(half):
        spans = []
        for slot, length in ((0, BLK), (1, BLK), (2, (half + 1) * edge_rows)):
            spans += [(slot, start, CHUNK) for start in range(0, length, CHUNK)]
        return spans

    for half in range(members // 2):

        @pl.when(group == half)
        def _(half=half):
            tops = [jnp.full((1, lanes), -FAR, jnp.float32)] * 3
            for span in spans_of(half):
                score(half, 0, even, span, tops)

            def body(index, tops):
                tops = tile(half, 2 * index, list(tops), even, odd)
                return tuple(tile(half, 2 * index + 1, tops, odd, even))

            lax.fori_loop(0, steps, body, tuple(tops))

    stores = [(query_done.at[place], out) for place, out in zip(places, query_outs)]
    if first:
        copies = run(stores + [(key_acc, acc_outs[0]), (value_acc, acc_outs[1])], out_sem)
        for copy in copies:
            copy.wait()
        return
    far_done, own_done, blank, far_sem = take[15:]
    copies = run(stores, out_sem)
    blank[...] = jnp.zeros_like(blank)
    shape = (members, rows, feature)
    for slot in range(2):
        span = slice(slot * BLK, (slot + 1) * BLK)
        far_done[slot, 0] = (key_acc[span] * factor).astype(jnp.bfloat16).reshape(shape)
        far_done[slot, 1] = value_acc[span].astype(jnp.bfloat16).reshape(shape)
    for hop in range(1, reach + 1):
        target = far_outs[hop - 1]
        for slot in range(2):

            @pl.when(offsets[slot] == hop)
            def _(target=target, slot=slot, hop=hop):
                pltpu.make_async_copy(far_done.at[slot], target, far_sem.at[hop]).start()

        @pl.when((offsets[0] != hop) & (offsets[1] != hop))
        def _(target=target, hop=hop):
            pltpu.make_async_copy(blank, target, far_sem.at[hop]).start()

    own_done[0] = (key_acc[2 * BLK :] * factor).reshape(shape)
    own_done[1] = value_acc[2 * BLK :].reshape(shape)
    for hop in range(members):
        copy = pltpu.make_async_copy(
            own_done.at[:, mine ^ hop], own_out.at[:, hop], out_sem.at[2 + hop]
        )
        copy.start()
        copies.append(copy)
    for copy in copies:
        copy.wait()
    for hop in range(1, reach + 1):
        pltpu.make_async_copy(blank, far_outs[hop - 1], far_sem.at[hop]).wait()


def attend(meta, inputs, near, far, sizes, first):
    members, reach, heads, rows, feature = sizes
    low, wide = jnp.bfloat16, jnp.float32
    pair = (2, members, rows, feature)
    acc = (3 * BLK, feature)
    anywhere = pl.BlockSpec(memory_space=pl.ANY)
    outs = [jax.ShapeDtypeStruct((heads, rows, feature), low)] * 2
    scratch = [
        pltpu.VMEM((2, heads, rows, feature), low),
        pltpu.VMEM((2, heads, rows, feature), low),
        pltpu.VMEM((2, heads, rows), low),
        pltpu.VMEM((2, heads, rows), wide),
        pltpu.VMEM((3,) + pair, low),
        pltpu.VMEM(acc, wide),
        pltpu.VMEM(acc, wide),
        pltpu.VMEM((2, heads, rows, feature), low),
        pltpu.SemaphoreType.DMA((members + 8,)),
        pltpu.SemaphoreType.DMA((2,)),
        pltpu.SemaphoreType.DMA((members + 2,)),
        pltpu.VMEM((3 * BLK, TILE_HEADS * rows), wide),
        pltpu.VMEM((3 * BLK, TILE_HEADS * rows), wide),
        pltpu.VMEM((3 * BLK, TILE_HEADS * rows), wide),
        pltpu.VMEM((3, feature, BLK), low),
    ]
    if first:
        outs += [jax.ShapeDtypeStruct(acc, wide)] * 2
    else:
        outs += [jax.ShapeDtypeStruct(pair, low)] * reach + [jax.ShapeDtypeStruct(pair, wide)]
        scratch += [
            pltpu.VMEM((2,) + pair, low),
            pltpu.VMEM(pair, wide),
            pltpu.VMEM(pair, low),
            pltpu.SemaphoreType.DMA((reach + 1,)),
        ]
    work = heads * 2 * rows * (2 * BLK + 3 * rows)
    return pl.pallas_call(
        functools.partial(attend_kernel, sizes, first),
        out_shape=outs,
        in_specs=[pl.BlockSpec(memory_space=pltpu.SMEM)]
        + [anywhere] * (len(inputs) + 1 + reach),
        out_specs=[anywhere] * len(outs),
        scratch_shapes=scratch,
        cost_estimate=pl.CostEstimate(
            flops=10 * work * feature, transcendentals=work, bytes_accessed=6 * 1024 * 1024
        ),
        compiler_params=pltpu.CompilerParams(vmem_limit_bytes=32 * 1024 * 1024),
    )(meta, *inputs, near, *far)


def settle_kernel(members, heads, meta, *refs):
    query_parts, pair_parts = refs[:members], refs[members : 2 * members]
    query_out, key_out, value_out, sem = refs[2 * members :]
    mine = meta[0]
    copies = []
    for hop in range(members):
        owner = mine ^ hop
        for source, target in (
            (query_parts[hop], query_out.at[0, pl.ds(owner * heads, heads)]),
            (pair_parts[hop].at[0], key_out.at[0, owner]),
            (pair_parts[hop].at[1], value_out.at[0, owner]),
        ):
            copy = pltpu.make_async_copy(source, target, sem)
            copy.start()
            copies.append(copy)
    for copy in copies:
        copy.wait()


def settle(meta, query_parts, pair_parts, shapes):
    members = len(query_parts)
    heads = query_parts[0].shape[0]
    anywhere = pl.BlockSpec(memory_space=pl.ANY)
    return pl.pallas_call(
        functools.partial(settle_kernel, members, heads),
        out_shape=[jax.ShapeDtypeStruct(shape, jnp.bfloat16) for shape in shapes],
        in_specs=[pl.BlockSpec(memory_space=pltpu.SMEM)]
        + [anywhere] * (2 * members),
        out_specs=[anywhere] * 3,
        scratch_shapes=[pltpu.SemaphoreType.DMA],
        compiler_params=pltpu.CompilerParams(vmem_limit_bytes=1024 * 1024),
    )(meta, *query_parts, *pair_parts)


def on_device(queries, key_states, value_states, outputs, out_grads, selected):
    devices = lax.axis_size("seq")
    sections = lax.axis_size("pipe")
    head_count, rows, feature = queries.shape[1:]
    key_heads = key_states.shape[1]
    members = BLK // rows
    heads = head_count // key_heads
    reach = devices // members - 1
    assert members == 4 and key_heads == 4 and heads % 8 == 0
    rank = lax.axis_index("seq")
    mine = rank % members
    block = rank // members

    def around(tensor, hop):
        return lax.ppermute(tensor, "seq", [(i, i ^ hop) for i in range(devices)])

    def along(tensor, hop):
        step = members * hop
        route = [(i, i + step) for i in range(devices) if 0 <= i + step < devices]
        return lax.ppermute(tensor, "seq", route)

    def previous(tensor, hop):
        route = [
            (i * sections + s, (i ^ hop) * sections + s - 1)
            for i in range(devices)
            for s in range(1, sections)
        ]
        return lax.ppermute(tensor, ("seq", "pipe"), route)

    chosen = lax.dynamic_slice(selected, (0, block, mine, 0), (1, 1, 1, 2)).reshape(2)
    usable = chosen < block
    offsets = jnp.where(usable, block - chosen, 0)
    meta = jnp.concatenate([mine[None], offsets]).astype(jnp.int32)

    def pair_of(hop):
        return jnp.concatenate(
            [
                lax.dynamic_slice_in_dim(states[0], mine ^ hop, 1, 0)
                for states in (key_states, value_states)
            ],
            axis=0,
        )

    deltas = jnp.sum(
        out_grads[0].astype(jnp.float32) * outputs[0].astype(jnp.float32), axis=-1
    ).astype(jnp.bfloat16)
    deltas = deltas.reshape(key_heads, heads, rows)

    def pack_of(hop):
        other = mine ^ hop
        query_part = lax.dynamic_slice_in_dim(queries[0], other * heads, heads, 0)
        grad_part = lax.dynamic_slice_in_dim(out_grads[0], other * heads, heads, 0)
        extra = lax.dynamic_index_in_dim(deltas, other, axis=0, keepdims=True)
        extra = jnp.pad(extra, ((0, 0), (0, rows - heads), (0, 0)))
        if hop == 1:
            extra = lax.optimization_barrier(jnp.concatenate([extra, pair_of(hop)], axis=0))
        return jnp.concatenate([query_part, grad_part, extra], axis=0)

    sides = [around(pair_of(hop), hop) for hop in range(2, members)]
    packs = [around(pack_of(hop), hop) for hop in range(1, members)]
    pieces = [pair_of(0), packs[0][2 * heads + 1 :]] + sides
    near = jnp.stack(pieces, axis=1)
    far = [along(near, hop) for hop in range(1, reach + 1)]

    sizes = (members, reach, heads, rows, feature)
    inputs = [queries, out_grads, deltas, packs[0]]
    *early_parts, key_acc, value_acc = attend(meta, inputs, near, far, sizes, True)
    early = [previous(part, hop) for hop, part in enumerate(early_parts)]
    inputs = [packs[1], packs[2], key_acc, value_acc]
    results = attend(meta, inputs, near, far, sizes, False)
    late_parts, far_parts, own_part = results[:2], results[2:-1], results[-1]
    early, late_parts, far_parts = lax.optimization_barrier((early, late_parts, far_parts))
    far_back = [along(part, -hop - 1) for hop, part in enumerate(far_parts)]
    late = [previous(part, hop + 2) for hop, part in enumerate(late_parts)]
    summed = own_part
    for part in far_back:
        summed = summed + part.astype(jnp.float32)
    summed = summed.astype(jnp.bfloat16)
    pair_back = [previous(summed[:, hop], hop) for hop in range(members)]
    shapes = (queries.shape, key_states.shape, value_states.shape)
    return tuple(settle(meta, early + late, pair_back, shapes))


def solution(mesh):
    return jax.shard_map(
        on_device,
        mesh=mesh,
        in_specs=(
            P("pipe", None, "seq", None),
            P("pipe", None, "seq", None),
            P("pipe", None, "seq", None),
            P("pipe", None, "seq", None),
            P("pipe", None, "seq", None),
            P("pipe", None, None, None),
        ),
        out_specs=(
            P("pipe", None, "seq", None),
            P("pipe", None, "seq", None),
            P("pipe", None, "seq", None),
        ),
        check_vma=False,
    )
```

```python
import functools
import math

import jax
import jax.numpy as jnp
from jax import lax
from jax.experimental import pallas as pl
from jax.experimental.pallas import tpu as pltpu
from jax.sharding import PartitionSpec as P

BLK = 512
TILE_HEADS = 2
CHUNK = 512
FAR = 1e30


def nt(a, b):
    return lax.dot_general(a, b, (((1,), (1,)), ((), ())), preferred_element_type=jnp.float32)


def nn(a, b):
    return lax.dot_general(a, b, (((1,), (0,)), ((), ())), preferred_element_type=jnp.float32)


def tn(a, b):
    return lax.dot_general(a, b, (((0,), (0,)), ((), ())), preferred_element_type=jnp.float32)


def attend_kernel(sizes, first, meta, *refs):
    members, reach, heads, rows, feature = sizes
    take = list(refs)
    if first:
        queries, grads, deltas, pack = take[:4]
        near, far, take = take[4], take[5 : 5 + reach], take[5 + reach :]
        query_outs, acc_outs, take = take[:2], take[2:4], take[4:]
    else:
        packs, acc_ins = take[:2], take[2:4]
        near, far, take = take[4], take[5 : 5 + reach], take[5 + reach :]
        query_outs, take = take[:2], take[2:]
        far_outs, own_out, take = take[:reach], take[reach], take[reach + 1 :]
    query_buf, grad_buf, low_buf, delta_buf, pair_buf, key_acc, value_acc, query_done = take[:8]
    in_sem, pair_sem, out_sem, even, odd, dprobs_buf, turned = take[8:15]
    mine = meta[0]
    offsets = (meta[1], meta[2])
    lanes = TILE_HEADS * rows
    factor = feature ** (-0.5)
    sharp = factor * math.log2(math.e)
    group = mine // 2 if first else 1 - mine // 2
    places = [mine % 2, 1 - mine % 2]

    def run(pairs, sems):
        copies = [
            pltpu.make_async_copy(source, target, sems.at[i])
            for i, (source, target) in enumerate(pairs)
        ]
        for copy in copies:
            copy.start()
        return copies

    def of_pack(pack, place):
        return [
            (pack.at[pl.ds(0, heads)], query_buf.at[place]),
            (pack.at[pl.ds(heads, heads)], grad_buf.at[place]),
            (pack.at[2 * heads, pl.ds(0, heads)], low_buf.at[place]),
        ]

    loads = [(near.at[:, hop], pair_buf.at[2, :, mine ^ hop]) for hop in range(members)]
    if first:
        span = pl.ds(mine * heads, heads)
        loads += [
            (queries.at[0, span], query_buf.at[places[0]]),
            (grads.at[0, span], grad_buf.at[places[0]]),
            (deltas.at[mine], low_buf.at[places[0]]),
        ]
        loads += of_pack(pack, places[1])
        key_acc[...] = jnp.zeros_like(key_acc)
        value_acc[...] = jnp.zeros_like(value_acc)
    else:
        loads += of_pack(packs[0], places[0]) + of_pack(packs[1], places[1])
        loads += [(acc_ins[0], key_acc), (acc_ins[1], value_acc)]
    copies = run(loads, in_sem)
    for slot in range(2):
        for hop in range(reach + 1):
            source = near if hop == 0 else far[hop - 1]

            @pl.when(offsets[slot] == hop)
            def _(source=source, slot=slot):
                pltpu.make_async_copy(source, pair_buf.at[slot], pair_sem.at[slot]).start()

    for copy in copies:
        copy.wait()
    for slot in range(2):
        pltpu.make_async_copy(near, pair_buf.at[slot], pair_sem.at[slot]).wait()
    delta_buf[...] = low_buf[...].astype(jnp.float32)

    biases = [jnp.where(offset > 0, 0.0, FAR) for offset in offsets]

    steps = heads // TILE_HEADS
    edge_rows = 2 * rows
    for slot in range(3):
        turned[slot] = pair_buf[slot, 0].reshape(BLK, feature).T

    def fetch(part, slot, start, size):
        return pair_buf[slot, part].reshape(BLK, feature)[start : start + size]

    def rows_of(buffer, place, step):
        return buffer[place, pl.ds(step * TILE_HEADS, TILE_HEADS)].reshape(lanes, feature)

    def score(half, index, buffer, span, tops):
        slot, start, size = span
        place, step = index // steps, index % steps
        part = nt(fetch(0, slot, start, size), rows_of(query_buf, place, step))
        if slot == 2 and start + size > half * edge_rows:
            key_ids = lax.broadcasted_iota(jnp.int32, (size, lanes), 0) + start
            row_ids = lax.broadcasted_iota(jnp.int32, (size, lanes), 1) % rows
            part = jnp.where(key_ids <= row_ids + (2 * half + place) * rows, part, -FAR)
        base = slot * BLK + start
        buffer[base : base + size] = part
        tops[slot] = jnp.maximum(tops[slot], jnp.max(part, axis=0, keepdims=True))

    def tile(half, index, tops, now, later):
        place, step = index // steps, index % steps
        query = rows_of(query_buf, place, step)
        grad = rows_of(grad_buf, place, step)
        delta = jnp.concatenate(
            [
                delta_buf[place, pl.ds(step * TILE_HEADS + i, 1), :]
                for i in range(TILE_HEADS)
            ],
            axis=1,
        )
        spans = spans_of(half)
        top = jnp.maximum(jnp.maximum(tops[0] - biases[0], tops[1] - biases[1]), tops[2])
        shifts = [top + biases[0], top + biases[1], top]
        total = jnp.zeros((1, lanes), jnp.float32)
        fresh = [jnp.full((1, lanes), -FAR, jnp.float32)] * 3
        for span in spans:
            slot, start, size = span
            base = slot * BLK + start
            score(half, jnp.minimum(index + 1, 2 * steps - 1), later, span, fresh)
            dprobs_buf[base : base + size] = nt(fetch(1, slot, start, size), grad)
            raw = jnp.exp2((now[base : base + size] - shifts[slot]) * sharp)
            now[base : base + size] = raw
            total += jnp.sum(raw, axis=0, keepdims=True)
        inverse = 1.0 / total
        query_sum = jnp.zeros((feature, lanes), jnp.float32)
        held = None
        for span in spans + [None]:
            if span is not None:
                slot, start, size = span
                base = slot * BLK + start
                probs = now[base : base + size] * inverse
                dscores = (probs * (dprobs_buf[base : base + size] - delta)).astype(jnp.bfloat16)
                waiting = (base, size, slot, start, probs.astype(jnp.bfloat16), dscores)
            if held is not None:
                base, size, slot, start, probs_low, dscores = held
                value_acc[base : base + size] += nn(probs_low, grad)
                key_acc[base : base + size] += nn(dscores, query)
                query_sum += nn(turned[slot][:, start : start + size], dscores)
            held = waiting
        query_done[place, pl.ds(step * TILE_HEADS, TILE_HEADS)] = (
            (query_sum.T * factor).astype(jnp.bfloat16).reshape(TILE_HEADS, rows, feature)
        )
        return fresh

    def spans_of(half):
        spans = []
        for slot, length in ((0, BLK), (1, BLK), (2, (half + 1) * edge_rows)):
            size = min(CHUNK, length)
            spans += [(slot, start, size) for start in range(0, length, size)]
        return spans

    for half in range(members // 2):

        @pl.when(group == half)
        def _(half=half):
            tops = [jnp.full((1, lanes), -FAR, jnp.float32)] * 3
            for span in spans_of(half):
                score(half, 0, even, span, tops)

            def body(index, tops):
                tops = tile(half, 2 * index, list(tops), even, odd)
                return tuple(tile(half, 2 * index + 1, tops, odd, even))

            lax.fori_loop(0, steps, body, tuple(tops))

    stores = [(query_done.at[place], out) for place, out in zip(places, query_outs)]
    if first:
        copies = run(stores + [(key_acc, acc_outs[0]), (value_acc, acc_outs[1])], out_sem)
        for copy in copies:
            copy.wait()
        return
    far_done, own_done, blank, far_sem = take[15:]
    copies = run(stores, out_sem)
    blank[...] = jnp.zeros_like(blank)
    shape = (members, rows, feature)
    for slot in range(2):
        span = slice(slot * BLK, (slot + 1) * BLK)
        far_done[slot, 0] = (key_acc[span] * factor).astype(jnp.bfloat16).reshape(shape)
        far_done[slot, 1] = value_acc[span].astype(jnp.bfloat16).reshape(shape)
    for hop in range(1, reach + 1):
        target = far_outs[hop - 1]
        for slot in range(2):

            @pl.when(offsets[slot] == hop)
            def _(target=target, slot=slot, hop=hop):
                pltpu.make_async_copy(far_done.at[slot], target, far_sem.at[hop]).start()

        @pl.when((offsets[0] != hop) & (offsets[1] != hop))
        def _(target=target, hop=hop):
            pltpu.make_async_copy(blank, target, far_sem.at[hop]).start()

    own_done[0] = (key_acc[2 * BLK :] * factor).reshape(shape)
    own_done[1] = value_acc[2 * BLK :].reshape(shape)
    for hop in range(members):
        copy = pltpu.make_async_copy(
            own_done.at[:, mine ^ hop], own_out.at[:, hop], out_sem.at[2 + hop]
        )
        copy.start()
        copies.append(copy)
    for copy in copies:
        copy.wait()
    for hop in range(1, reach + 1):
        pltpu.make_async_copy(blank, far_outs[hop - 1], far_sem.at[hop]).wait()


def attend(meta, inputs, near, far, sizes, first):
    members, reach, heads, rows, feature = sizes
    low, wide = jnp.bfloat16, jnp.float32
    pair = (2, members, rows, feature)
    acc = (3 * BLK, feature)
    anywhere = pl.BlockSpec(memory_space=pl.ANY)
    outs = [jax.ShapeDtypeStruct((heads, rows, feature), low)] * 2
    scratch = [
        pltpu.VMEM((2, heads, rows, feature), low),
        pltpu.VMEM((2, heads, rows, feature), low),
        pltpu.VMEM((2, heads, rows), low),
        pltpu.VMEM((2, heads, rows), wide),
        pltpu.VMEM((3,) + pair, low),
        pltpu.VMEM(acc, wide),
        pltpu.VMEM(acc, wide),
        pltpu.VMEM((2, heads, rows, feature), low),
        pltpu.SemaphoreType.DMA((members + 8,)),
        pltpu.SemaphoreType.DMA((2,)),
        pltpu.SemaphoreType.DMA((members + 2,)),
        pltpu.VMEM((3 * BLK, TILE_HEADS * rows), wide),
        pltpu.VMEM((3 * BLK, TILE_HEADS * rows), wide),
        pltpu.VMEM((3 * BLK, TILE_HEADS * rows), wide),
        pltpu.VMEM((3, feature, BLK), low),
    ]
    if first:
        outs += [jax.ShapeDtypeStruct(acc, wide)] * 2
    else:
        outs += [jax.ShapeDtypeStruct(pair, low)] * reach + [jax.ShapeDtypeStruct(pair, wide)]
        scratch += [
            pltpu.VMEM((2,) + pair, low),
            pltpu.VMEM(pair, wide),
            pltpu.VMEM(pair, low),
            pltpu.SemaphoreType.DMA((reach + 1,)),
        ]
    work = heads * 2 * rows * (2 * BLK + 3 * rows)
    return pl.pallas_call(
        functools.partial(attend_kernel, sizes, first),
        out_shape=outs,
        in_specs=[pl.BlockSpec(memory_space=pltpu.SMEM)]
        + [anywhere] * (len(inputs) + 1 + reach),
        out_specs=[anywhere] * len(outs),
        scratch_shapes=scratch,
        cost_estimate=pl.CostEstimate(
            flops=10 * work * feature, transcendentals=work, bytes_accessed=6 * 1024 * 1024
        ),
        compiler_params=pltpu.CompilerParams(vmem_limit_bytes=32 * 1024 * 1024),
    )(meta, *inputs, near, *far)


def settle_kernel(members, heads, meta, *refs):
    query_parts, pair_parts = refs[:members], refs[members : 2 * members]
    query_out, key_out, value_out, sem = refs[2 * members :]
    mine = meta[0]
    copies = []
    for hop in range(members):
        owner = mine ^ hop
        for source, target in (
            (query_parts[hop], query_out.at[0, pl.ds(owner * heads, heads)]),
            (pair_parts[hop].at[0], key_out.at[0, owner]),
            (pair_parts[hop].at[1], value_out.at[0, owner]),
        ):
            copy = pltpu.make_async_copy(source, target, sem)
            copy.start()
            copies.append(copy)
    for copy in copies:
        copy.wait()


def settle(meta, query_parts, pair_parts, shapes):
    members = len(query_parts)
    heads = query_parts[0].shape[0]
    anywhere = pl.BlockSpec(memory_space=pl.ANY)
    return pl.pallas_call(
        functools.partial(settle_kernel, members, heads),
        out_shape=[jax.ShapeDtypeStruct(shape, jnp.bfloat16) for shape in shapes],
        in_specs=[pl.BlockSpec(memory_space=pltpu.SMEM)]
        + [anywhere] * (2 * members),
        out_specs=[anywhere] * 3,
        scratch_shapes=[pltpu.SemaphoreType.DMA],
        compiler_params=pltpu.CompilerParams(vmem_limit_bytes=1024 * 1024),
    )(meta, *query_parts, *pair_parts)


def on_device(queries, key_states, value_states, outputs, out_grads, selected):
    devices = lax.axis_size("seq")
    sections = lax.axis_size("pipe")
    head_count, rows, feature = queries.shape[1:]
    key_heads = key_states.shape[1]
    members = BLK // rows
    heads = head_count // key_heads
    reach = devices // members - 1
    assert members == 4 and key_heads == 4 and heads % 8 == 0
    rank = lax.axis_index("seq")
    mine = rank % members
    block = rank // members

    def around(tensor, hop):
        return lax.ppermute(tensor, "seq", [(i, i ^ hop) for i in range(devices)])

    def along(tensor, hop):
        step = members * hop
        route = [(i, i + step) for i in range(devices) if 0 <= i + step < devices]
        return lax.ppermute(tensor, "seq", route)

    def previous(tensor, hop):
        route = [
            (i * sections + s, (i ^ hop) * sections + s - 1)
            for i in range(devices)
            for s in range(1, sections)
        ]
        return lax.ppermute(tensor, ("seq", "pipe"), route)

    chosen = lax.dynamic_slice(selected, (0, block, mine, 0), (1, 1, 1, 2)).reshape(2)
    usable = chosen < block
    offsets = jnp.where(usable, block - chosen, 0)
    meta = jnp.concatenate([mine[None], offsets]).astype(jnp.int32)

    def pair_of(hop):
        return jnp.concatenate(
            [
                lax.dynamic_slice_in_dim(states[0], mine ^ hop, 1, 0)
                for states in (key_states, value_states)
            ],
            axis=0,
        )

    deltas = jnp.sum(
        out_grads[0].astype(jnp.float32) * outputs[0].astype(jnp.float32), axis=-1
    ).astype(jnp.bfloat16)
    deltas = deltas.reshape(key_heads, heads, rows)

    def pack_of(hop):
        other = mine ^ hop
        query_part = lax.dynamic_slice_in_dim(queries[0], other * heads, heads, 0)
        grad_part = lax.dynamic_slice_in_dim(out_grads[0], other * heads, heads, 0)
        extra = lax.dynamic_index_in_dim(deltas, other, axis=0, keepdims=True)
        extra = jnp.pad(extra, ((0, 0), (0, rows - heads), (0, 0)))
        if hop == 1:
            extra = lax.optimization_barrier(jnp.concatenate([extra, pair_of(hop)], axis=0))
        return jnp.concatenate([query_part, grad_part, extra], axis=0)

    sides = [around(pair_of(hop), hop) for hop in range(2, members)]
    packs = [around(pack_of(hop), hop) for hop in range(1, members)]
    pieces = [pair_of(0), packs[0][2 * heads + 1 :]] + sides
    near = jnp.stack(pieces, axis=1)
    far = [along(near, hop) for hop in range(1, reach + 1)]

    sizes = (members, reach, heads, rows, feature)
    inputs = [queries, out_grads, deltas, packs[0]]
    *early_parts, key_acc, value_acc = attend(meta, inputs, near, far, sizes, True)
    early = [previous(part, hop) for hop, part in enumerate(early_parts)]
    inputs = [packs[1], packs[2], key_acc, value_acc]
    results = attend(meta, inputs, near, far, sizes, False)
    late_parts, far_parts, own_part = results[:2], results[2:-1], results[-1]
    early, late_parts, far_parts = lax.optimization_barrier((early, late_parts, far_parts))
    far_back = [along(part, -hop - 1) for hop, part in enumerate(far_parts)]
    late = [previous(part, hop + 2) for hop, part in enumerate(late_parts)]
    summed = own_part
    for part in far_back:
        summed = summed + part.astype(jnp.float32)
    summed = summed.astype(jnp.bfloat16)
    pair_back = [previous(summed[:, hop], hop) for hop in range(members)]
    shapes = (queries.shape, key_states.shape, value_states.shape)
    return tuple(settle(meta, early + late, pair_back, shapes))


def solution(mesh):
    return jax.shard_map(
        on_device,
        mesh=mesh,
        in_specs=(
            P("pipe", None, "seq", None),
            P("pipe", None, "seq", None),
            P("pipe", None, "seq", None),
            P("pipe", None, "seq", None),
            P("pipe", None, "seq", None),
            P("pipe", None, None, None),
        ),
        out_specs=(
            P("pipe", None, "seq", None),
            P("pipe", None, "seq", None),
            P("pipe", None, "seq", None),
        ),
        check_vma=False,
    )
```

```python
import functools
import math

import jax
import jax.numpy as jnp
from jax import lax
from jax.experimental import pallas as pl
from jax.experimental.pallas import tpu as pltpu
from jax.sharding import PartitionSpec as P

BLK = 512
TILE_HEADS = 2
CHUNK = 512
FAR = 1e30


def nt(a, b):
    return lax.dot_general(a, b, (((1,), (1,)), ((), ())), preferred_element_type=jnp.float32)


def nn(a, b):
    return lax.dot_general(a, b, (((1,), (0,)), ((), ())), preferred_element_type=jnp.float32)


def tn(a, b):
    return lax.dot_general(a, b, (((0,), (0,)), ((), ())), preferred_element_type=jnp.float32)


def attend_kernel(sizes, first, meta, *refs):
    members, reach, heads, rows, feature = sizes
    take = list(refs)
    if first:
        queries, grads, deltas, pack = take[:4]
        near, far, take = take[4], take[5 : 5 + reach], take[5 + reach :]
        query_outs, acc_outs, take = take[:2], take[2:4], take[4:]
    else:
        packs, acc_ins = take[:2], take[2:4]
        near, far, take = take[4], take[5 : 5 + reach], take[5 + reach :]
        query_outs, take = take[:2], take[2:]
        far_outs, own_out, take = take[:reach], take[reach], take[reach + 1 :]
    query_buf, grad_buf, low_buf, delta_buf, pair_buf, key_acc, value_acc, query_done = take[:8]
    in_sem, pair_sem, out_sem, even, odd, dprobs_buf, turned = take[8:15]
    mine = meta[0]
    offsets = (meta[1], meta[2])
    lanes = TILE_HEADS * rows
    factor = feature ** (-0.5)
    sharp = factor * math.log2(math.e)
    group = mine // 2 if first else 1 - mine // 2
    places = [mine % 2, 1 - mine % 2]

    def run(pairs, sems):
        copies = [
            pltpu.make_async_copy(source, target, sems.at[i])
            for i, (source, target) in enumerate(pairs)
        ]
        for copy in copies:
            copy.start()
        return copies

    def of_pack(pack, place):
        return [
            (pack.at[pl.ds(0, heads)], query_buf.at[place]),
            (pack.at[pl.ds(heads, heads)], grad_buf.at[place]),
            (pack.at[2 * heads, pl.ds(0, heads)], low_buf.at[place]),
        ]

    loads = [(near.at[:, hop], pair_buf.at[2, :, mine ^ hop]) for hop in range(members)]
    if first:
        span = pl.ds(mine * heads, heads)
        loads += [
            (queries.at[0, span], query_buf.at[places[0]]),
            (grads.at[0, span], grad_buf.at[places[0]]),
            (deltas.at[mine], low_buf.at[places[0]]),
        ]
        loads += of_pack(pack, places[1])
    else:
        loads += of_pack(packs[0], places[0]) + of_pack(packs[1], places[1])
    copies = run(loads, in_sem)
    if not first:
        key_more, value_more, more_sem = take[-3:]
        more_copies = run([(acc_ins[0], key_more), (acc_ins[1], value_more)], more_sem)
    key_acc[...] = jnp.zeros_like(key_acc)
    value_acc[...] = jnp.zeros_like(value_acc)
    for slot in range(2):
        for hop in range(reach + 1):
            source = near if hop == 0 else far[hop - 1]

            @pl.when(offsets[slot] == hop)
            def _(source=source, slot=slot):
                pltpu.make_async_copy(source, pair_buf.at[slot], pair_sem.at[slot]).start()

    for copy in copies:
        copy.wait()
    for slot in range(2):
        pltpu.make_async_copy(near, pair_buf.at[slot], pair_sem.at[slot]).wait()
    delta_buf[...] = low_buf[...].astype(jnp.float32)

    biases = [jnp.where(offset > 0, 0.0, FAR) for offset in offsets]

    steps = heads // TILE_HEADS
    edge_rows = 2 * rows
    for slot in range(3):
        turned[slot] = pair_buf[slot, 0].reshape(BLK, feature).T

    def fetch(part, slot, start, size):
        return pair_buf[slot, part].reshape(BLK, feature)[start : start + size]

    def rows_of(buffer, place, step):
        return buffer[place, pl.ds(step * TILE_HEADS, TILE_HEADS)].reshape(lanes, feature)

    def score(half, index, buffer, span, tops):
        slot, start, size = span
        place, step = index // steps, index % steps
        part = nt(fetch(0, slot, start, size), rows_of(query_buf, place, step))
        if slot == 2 and start + size > half * edge_rows:
            key_ids = lax.broadcasted_iota(jnp.int32, (size, lanes), 0) + start
            row_ids = lax.broadcasted_iota(jnp.int32, (size, lanes), 1) % rows
            part = jnp.where(key_ids <= row_ids + (2 * half + place) * rows, part, -FAR)
        base = slot * BLK + start
        buffer[base : base + size] = part
        tops[slot] = jnp.maximum(tops[slot], jnp.max(part, axis=0, keepdims=True))

    def tile(half, index, tops, now, later):
        place, step = index // steps, index % steps
        query = rows_of(query_buf, place, step)
        grad = rows_of(grad_buf, place, step)
        delta = jnp.concatenate(
            [
                delta_buf[place, pl.ds(step * TILE_HEADS + i, 1), :]
                for i in range(TILE_HEADS)
            ],
            axis=1,
        )
        spans = spans_of(half)
        top = jnp.maximum(jnp.maximum(tops[0] - biases[0], tops[1] - biases[1]), tops[2])
        shifts = [top + biases[0], top + biases[1], top]
        total = jnp.zeros((1, lanes), jnp.float32)
        fresh = [jnp.full((1, lanes), -FAR, jnp.float32)] * 3
        for span in spans:
            slot, start, size = span
            base = slot * BLK + start
            score(half, jnp.minimum(index + 1, 2 * steps - 1), later, span, fresh)
            dprobs_buf[base : base + size] = nt(fetch(1, slot, start, size), grad)
            raw = jnp.exp2((now[base : base + size] - shifts[slot]) * sharp)
            now[base : base + size] = raw
            total += jnp.sum(raw, axis=0, keepdims=True)
        inverse = 1.0 / total
        query_sum = jnp.zeros((feature, lanes), jnp.float32)
        held = None
        for span in spans + [None]:
            if span is not None:
                slot, start, size = span
                base = slot * BLK + start
                probs = now[base : base + size] * inverse
                dscores = (probs * (dprobs_buf[base : base + size] - delta)).astype(jnp.bfloat16)
                waiting = (base, size, slot, start, probs.astype(jnp.bfloat16), dscores)
            if held is not None:
                base, size, slot, start, probs_low, dscores = held
                value_acc[base : base + size] += nn(probs_low, grad)
                key_acc[base : base + size] += nn(dscores, query)
                query_sum += nn(turned[slot][:, start : start + size], dscores)
            held = waiting
        query_done[place, pl.ds(step * TILE_HEADS, TILE_HEADS)] = (
            (query_sum.T * factor).astype(jnp.bfloat16).reshape(TILE_HEADS, rows, feature)
        )
        return fresh

    def spans_of(half):
        spans = []
        for slot, length in ((0, BLK), (1, BLK), (2, (half + 1) * edge_rows)):
            size = min(CHUNK, length)
            spans += [(slot, start, size) for start in range(0, length, size)]
        return spans

    for half in range(members // 2):

        @pl.when(group == half)
        def _(half=half):
            tops = [jnp.full((1, lanes), -FAR, jnp.float32)] * 3
            for span in spans_of(half):
                score(half, 0, even, span, tops)

            def body(index, tops):
                tops = tile(half, 2 * index, list(tops), even, odd)
                return tuple(tile(half, 2 * index + 1, tops, odd, even))

            lax.fori_loop(0, steps, body, tuple(tops))

    stores = [(query_done.at[place], out) for place, out in zip(places, query_outs)]
    if first:
        copies = run(stores + [(key_acc, acc_outs[0]), (value_acc, acc_outs[1])], out_sem)
        for copy in copies:
            copy.wait()
        return
    far_done, own_done, blank, far_sem = take[15:19]
    copies = run(stores, out_sem)
    for copy in more_copies:
        copy.wait()
    key_acc[...] += key_more[...]
    value_acc[...] += value_more[...]
    blank[...] = jnp.zeros_like(blank)
    shape = (members, rows, feature)
    for slot in range(2):
        span = slice(slot * BLK, (slot + 1) * BLK)
        far_done[slot, 0] = (key_acc[span] * factor).astype(jnp.bfloat16).reshape(shape)
        far_done[slot, 1] = value_acc[span].astype(jnp.bfloat16).reshape(shape)
    for hop in range(1, reach + 1):
        target = far_outs[hop - 1]
        for slot in range(2):

            @pl.when(offsets[slot] == hop)
            def _(target=target, slot=slot, hop=hop):
                pltpu.make_async_copy(far_done.at[slot], target, far_sem.at[hop]).start()

        @pl.when((offsets[0] != hop) & (offsets[1] != hop))
        def _(target=target, hop=hop):
            pltpu.make_async_copy(blank, target, far_sem.at[hop]).start()

    own_done[0] = (key_acc[2 * BLK :] * factor).reshape(shape)
    own_done[1] = value_acc[2 * BLK :].reshape(shape)
    for hop in range(members):
        copy = pltpu.make_async_copy(
            own_done.at[:, mine ^ hop], own_out.at[:, hop], out_sem.at[2 + hop]
        )
        copy.start()
        copies.append(copy)
    for copy in copies:
        copy.wait()
    for hop in range(1, reach + 1):
        pltpu.make_async_copy(blank, far_outs[hop - 1], far_sem.at[hop]).wait()


def attend(meta, inputs, near, far, sizes, first):
    members, reach, heads, rows, feature = sizes
    low, wide = jnp.bfloat16, jnp.float32
    pair = (2, members, rows, feature)
    acc = (3 * BLK, feature)
    anywhere = pl.BlockSpec(memory_space=pl.ANY)
    outs = [jax.ShapeDtypeStruct((heads, rows, feature), low)] * 2
    scratch = [
        pltpu.VMEM((2, heads, rows, feature), low),
        pltpu.VMEM((2, heads, rows, feature), low),
        pltpu.VMEM((2, heads, rows), low),
        pltpu.VMEM((2, heads, rows), wide),
        pltpu.VMEM((3,) + pair, low),
        pltpu.VMEM(acc, wide),
        pltpu.VMEM(acc, wide),
        pltpu.VMEM((2, heads, rows, feature), low),
        pltpu.SemaphoreType.DMA((members + 8,)),
        pltpu.SemaphoreType.DMA((2,)),
        pltpu.SemaphoreType.DMA((members + 2,)),
        pltpu.VMEM((3 * BLK, TILE_HEADS * rows), wide),
        pltpu.VMEM((3 * BLK, TILE_HEADS * rows), wide),
        pltpu.VMEM((3 * BLK, TILE_HEADS * rows), wide),
        pltpu.VMEM((3, feature, BLK), low),
    ]
    if first:
        outs += [jax.ShapeDtypeStruct(acc, wide)] * 2
    else:
        outs += [jax.ShapeDtypeStruct(pair, low)] * reach + [jax.ShapeDtypeStruct(pair, wide)]
        scratch += [
            pltpu.VMEM((2,) + pair, low),
            pltpu.VMEM(pair, wide),
            pltpu.VMEM(pair, low),
            pltpu.SemaphoreType.DMA((reach + 1,)),
            pltpu.VMEM(acc, wide),
            pltpu.VMEM(acc, wide),
            pltpu.SemaphoreType.DMA((2,)),
        ]
    work = heads * 2 * rows * (2 * BLK + 3 * rows)
    return pl.pallas_call(
        functools.partial(attend_kernel, sizes, first),
        out_shape=outs,
        in_specs=[pl.BlockSpec(memory_space=pltpu.SMEM)]
        + [anywhere] * (len(inputs) + 1 + reach),
        out_specs=[anywhere] * len(outs),
        scratch_shapes=scratch,
        cost_estimate=pl.CostEstimate(
            flops=10 * work * feature, transcendentals=work, bytes_accessed=6 * 1024 * 1024
        ),
        compiler_params=pltpu.CompilerParams(vmem_limit_bytes=22 * 1024 * 1024),
    )(meta, *inputs, near, *far)


def settle_kernel(members, heads, meta, *refs):
    query_parts, pair_parts = refs[:members], refs[members : 2 * members]
    query_out, key_out, value_out, sem = refs[2 * members :]
    mine = meta[0]
    copies = []
    for hop in range(members):
        owner = mine ^ hop
        for source, target in (
            (query_parts[hop], query_out.at[0, pl.ds(owner * heads, heads)]),
            (pair_parts[hop].at[0], key_out.at[0, owner]),
            (pair_parts[hop].at[1], value_out.at[0, owner]),
        ):
            copy = pltpu.make_async_copy(source, target, sem)
            copy.start()
            copies.append(copy)
    for copy in copies:
        copy.wait()


def settle(meta, query_parts, pair_parts, shapes):
    members = len(query_parts)
    heads = query_parts[0].shape[0]
    anywhere = pl.BlockSpec(memory_space=pl.ANY)
    return pl.pallas_call(
        functools.partial(settle_kernel, members, heads),
        out_shape=[jax.ShapeDtypeStruct(shape, jnp.bfloat16) for shape in shapes],
        in_specs=[pl.BlockSpec(memory_space=pltpu.SMEM)]
        + [anywhere] * (2 * members),
        out_specs=[anywhere] * 3,
        scratch_shapes=[pltpu.SemaphoreType.DMA],
        compiler_params=pltpu.CompilerParams(vmem_limit_bytes=1024 * 1024),
    )(meta, *query_parts, *pair_parts)


def on_device(queries, key_states, value_states, outputs, out_grads, selected):
    devices = lax.axis_size("seq")
    sections = lax.axis_size("pipe")
    head_count, rows, feature = queries.shape[1:]
    key_heads = key_states.shape[1]
    members = BLK // rows
    heads = head_count // key_heads
    reach = devices // members - 1
    assert members == 4 and key_heads == 4 and heads % 8 == 0
    rank = lax.axis_index("seq")
    mine = rank % members
    block = rank // members

    def around(tensor, hop):
        return lax.ppermute(tensor, "seq", [(i, i ^ hop) for i in range(devices)])

    def along(tensor, hop):
        step = members * hop
        route = [(i, i + step) for i in range(devices) if 0 <= i + step < devices]
        return lax.ppermute(tensor, "seq", route)

    def previous(tensor, hop):
        route = [
            (i * sections + s, (i ^ hop) * sections + s - 1)
            for i in range(devices)
            for s in range(1, sections)
        ]
        return lax.ppermute(tensor, ("seq", "pipe"), route)

    chosen = lax.dynamic_slice(selected, (0, block, mine, 0), (1, 1, 1, 2)).reshape(2)
    usable = chosen < block
    offsets = jnp.where(usable, block - chosen, 0)
    meta = jnp.concatenate([mine[None], offsets]).astype(jnp.int32)

    def pair_of(hop):
        return jnp.concatenate(
            [
                lax.dynamic_slice_in_dim(states[0], mine ^ hop, 1, 0)
                for states in (key_states, value_states)
            ],
            axis=0,
        )

    deltas = jnp.sum(
        out_grads[0].astype(jnp.float32) * outputs[0].astype(jnp.float32), axis=-1
    ).astype(jnp.bfloat16)
    deltas = deltas.reshape(key_heads, heads, rows)

    def pack_of(hop):
        other = mine ^ hop
        query_part = lax.dynamic_slice_in_dim(queries[0], other * heads, heads, 0)
        grad_part = lax.dynamic_slice_in_dim(out_grads[0], other * heads, heads, 0)
        extra = lax.dynamic_index_in_dim(deltas, other, axis=0, keepdims=True)
        extra = jnp.pad(extra, ((0, 0), (0, rows - heads), (0, 0)))
        if hop == 1:
            extra = lax.optimization_barrier(jnp.concatenate([extra, pair_of(hop)], axis=0))
        return jnp.concatenate([query_part, grad_part, extra], axis=0)

    sides = [around(pair_of(hop), hop) for hop in range(2, members)]
    packs = [around(pack_of(hop), hop) for hop in range(1, members)]
    pieces = [pair_of(0), packs[0][2 * heads + 1 :]] + sides
    near = jnp.stack(pieces, axis=1)
    far = [along(near, hop) for hop in range(1, reach + 1)]

    sizes = (members, reach, heads, rows, feature)
    inputs = [queries, out_grads, deltas, packs[0]]
    *early_parts, key_acc, value_acc = attend(meta, inputs, near, far, sizes, True)
    early = [previous(part, hop) for hop, part in enumerate(early_parts)]
    inputs = [packs[1], packs[2], key_acc, value_acc]
    results = attend(meta, inputs, near, far, sizes, False)
    late_parts, far_parts, own_part = results[:2], results[2:-1], results[-1]
    early, late_parts, far_parts = lax.optimization_barrier((early, late_parts, far_parts))
    far_back = [along(part, -hop - 1) for hop, part in enumerate(far_parts)]
    late = [previous(part, hop + 2) for hop, part in enumerate(late_parts)]
    summed = own_part
    for part in far_back:
        summed = summed + part.astype(jnp.float32)
    summed = summed.astype(jnp.bfloat16)
    pair_back = [previous(summed[:, hop], hop) for hop in range(members)]
    shapes = (queries.shape, key_states.shape, value_states.shape)
    return tuple(settle(meta, early + late, pair_back, shapes))


def solution(mesh):
    return jax.shard_map(
        on_device,
        mesh=mesh,
        in_specs=(
            P("pipe", None, "seq", None),
            P("pipe", None, "seq", None),
            P("pipe", None, "seq", None),
            P("pipe", None, "seq", None),
            P("pipe", None, "seq", None),
            P("pipe", None, None, None),
        ),
        out_specs=(
            P("pipe", None, "seq", None),
            P("pipe", None, "seq", None),
            P("pipe", None, "seq", None),
        ),
        check_vma=False,
    )
```
